512 devices in a mesh: freq: 32 (over z, x), bfly: 16 (over y, core).
Axes of the slice: x: 4, y: 8, z: 8, core: 2. Of those that a mesh axis runs over, the one named last changes fastest.
Arguments:
- sources: bfloat16 [2, 2048, 8192], P(None, 'bfly', 'freq'), may hold values from -6 to 6
- observed: bfloat16 [2, 2048, 8192], P(None, 'bfly', 'freq'), may hold values from -4 to 4
- receivers: int32 [2048], P('bfly'), may hold values from 0 to 127
- model: float32 [2048], P('bfly'), may hold values from 0.25 to 1.75
- phases: float32 [4, 2048, 128], P(None, 'bfly', 'freq'), may hold values from -3.140625 to 3.140625
- near_blocks: bfloat16 [4, 2, 2048, 128], P(None, None, 'bfly'), may hold values from -0.25 to 0.25
- far_blocks: bfloat16 [4, 2, 2048, 128], P(None, None, 'bfly'), may hold values from -0.25 to 0.25
- pattern: int32 [4, 2, 32, 2], P(None, None, 'bfly'), may hold values 0 or 1
Outputs:
- gradient: float32 [2048], P('bfly')
- residual: float32 [2, 2048, 8192], P(None, 'bfly', 'freq')
The draws below stay inside these ranges and needn't reach their ends.
Inputs may be any that keep to these rules, and one draw needn't show every extreme that they name: `receivers`: entries may repeat; receiver j belongs to block j // 128.
All inputs are finite; a program needn't handle non-finite values. No bound on the sum of `pattern` on one device may be relied on, other than what follows from the above.
Results may differ from the reference program's by a relative error of at most 0.0055.
Values may be sent and summed in bfloat16 or wider, within the bound.
No kernel may reach another device: no remote copies, remote signals or barrier semaphores. Data moves between devices by JAX's collectives and lax.ppermute only.
A program may use at most 64 MiB of HBM per device.

```python
import jax
import jax.numpy as jnp
import numpy as np
from jax import lax

RANK = 64
K = 64
NREC = 128
LEVELS = 4
R = 128
ROWS = 2048
NF = 128
RECV = 2048
N_BFLY = 16


def set_ends(values, rng, least, top_value):
    place = [jax.random.randint(jax.random.fold_in(rng, axis), (), 0, length) for axis, length in enumerate(values.shape)]
    widest = values.shape.index(max(values.shape))
    neighbour = place[:widest] + [(place[widest] + 1) % values.shape[widest]] + place[widest + 1:]
    return values.at[tuple(place)].set(least).at[tuple(neighbour)].set(top_value)


def block_levels(rng, extent, shards, least, top_value):
    level, own = 1.0, jax.random.fold_in(rng, 6)
    for dim, blocks in shards:
        heights = jnp.exp(jax.random.uniform(jax.random.fold_in(own, dim), (blocks,), jnp.float32, least / len(shards), top_value / len(shards)))
        level = level * jnp.repeat(heights, extent[dim] // blocks).reshape([-1 if axis == dim else 1 for axis in range(len(extent))])
    return level


def bell_draw(key, shape, width, limit, shards=(), held_as=jnp.bfloat16):
    entries = jax.random.normal(key, shape, jnp.float32) * width
    if len(shards) > 0:
        entries = block_levels(key, shape, shards, -0.22, 0.18) * entries
    return jnp.clip(entries, min=-limit, max=limit).astype(held_as)


def setup_inputs(seed: int = 0) -> dict:
    keys = jax.random.split(jax.random.key(seed), 9)
    return {
        "sources": bell_draw(keys[0], (2, ROWS, NF * K), 1.0, 6.0, ((1, 16), (2, 32))),
        "observed": bell_draw(keys[1], (2, RECV, NF * K), 0.5, 4.0, ((1, 16), (2, 32))),
        "receivers": set_ends(jax.random.randint(keys[2], (RECV,), 0, R), jax.random.fold_in(keys[2], 1), 0, R - 1).astype(jnp.int32),
        "model": jnp.clip(1.0 + 0.15 * jax.random.normal(keys[3], (ROWS,), jnp.float32), 0.25, 1.75),
        "phases": jnp.clip(jax.random.uniform(keys[4], (LEVELS, ROWS, NF), jnp.float32, -3.140625, 3.140625), -3.140625, 3.140625),
        "near_blocks": bell_draw(keys[5], (LEVELS, 2, ROWS, R), (4 * R) ** -0.5, 0.25, ((2, 16),)),
        "far_blocks": bell_draw(keys[6], (LEVELS, 2, ROWS, R), (4 * R) ** -0.5, 0.25, ((2, 16),)),
        "pattern": set_ends((jax.random.randint(keys[7], (LEVELS, 2, ROWS // RANK, R // RANK), 0, 4) < 3).astype(jnp.int32), jax.random.fold_in(keys[7], 1), 0, 1),
    }


epsilon = 1e-05

def rounded(values):
    return lax.optimization_barrier(values.astype(jnp.bfloat16)).astype(jnp.float32)

def forward_mul(blocks, values):
    real_part = jnp.einsum('brs,bsc->brc', blocks[0], values[0]) - jnp.einsum('brs,bsc->brc', blocks[1], values[1])
    imag_part = jnp.einsum('brs,bsc->brc', blocks[0], values[1]) + jnp.einsum('brs,bsc->brc', blocks[1], values[0])
    return jnp.stack([real_part, imag_part])

def adjoint_mul(blocks, values):
    real_part = jnp.einsum('bsr,bsc->brc', blocks[0], values[0]) + jnp.einsum('bsr,bsc->brc', blocks[1], values[1])
    imag_part = jnp.einsum('bsr,bsc->brc', blocks[0], values[1]) - jnp.einsum('bsr,bsc->brc', blocks[1], values[0])
    return jnp.stack([real_part, imag_part])

def expand(phases, level):
    angle = jnp.repeat(phases[level], K, axis=-1)
    return (jnp.cos(angle), jnp.sin(angle))

def reference(sources, observed, receivers, model, phases, near_blocks, far_blocks, pattern):
    columns = sources.shape[-1]
    mask = jnp.repeat(jnp.repeat(pattern, RANK, axis=2), RANK, axis=3).astype(jnp.float32)
    near = (near_blocks.astype(jnp.float32) * mask[:, 0:1]).reshape(LEVELS, 2, N_BFLY, R, R)
    far = (far_blocks.astype(jnp.float32) * mask[:, 1:2]).reshape(LEVELS, 2, N_BFLY, R, R)
    source_wide = sources.astype(jnp.float32)
    field = rounded(model[None, :, None] * source_wide)
    for level in range(LEVELS):
        values = field.reshape(2, N_BFLY, R, columns)
        partner = np.arange(N_BFLY) ^ 1 << level
        mixed = forward_mul(near[level], values) + forward_mul(far[level], values[:, partner])
        mixed = mixed.reshape(2, ROWS, columns)
        cosine, sine = expand(phases, level)
        field = rounded(jnp.stack([cosine * mixed[0] - sine * mixed[1], sine * mixed[0] + cosine * mixed[1]]))
    rows = jnp.arange(RECV, dtype=jnp.int32) // NREC * R + receivers.astype(jnp.int32)
    picked = field[:, rows]
    residual = picked - observed.astype(jnp.float32)
    back = jnp.zeros((2, ROWS, columns), jnp.float32).at[:, rows].add(rounded(residual))
    adjoint = rounded(back)
    for level in reversed(range(LEVELS)):
        partner = np.arange(N_BFLY) ^ 1 << level
        cosine, sine = expand(phases, level)
        turned = rounded(jnp.stack([cosine * adjoint[0] + sine * adjoint[1], cosine * adjoint[1] - sine * adjoint[0]]))
        turned = turned.reshape(2, N_BFLY, R, columns)
        local_term = adjoint_mul(near[level], turned)
        far_term = rounded(adjoint_mul(far[level], turned))[:, partner]
        adjoint = rounded((local_term + far_term).reshape(2, ROWS, columns))
    gradient_part = lax.optimization_barrier(jnp.sum(source_wide[0] * adjoint[0] + source_wide[1] * adjoint[1], axis=-1))
    illumination = lax.optimization_barrier(jnp.sum(source_wide[0] * source_wide[0] + source_wide[1] * source_wide[1], axis=-1))
    gradient = gradient_part / jnp.sqrt(illumination + epsilon)
    return (gradient, residual)
```

```python
import jax
import jax.numpy as jnp
from jax import lax
from jax.sharding import PartitionSpec as P

epsilon = 1e-05


def swapped(block, stride):
    count = lax.axis_size("bfly")
    route = [(place, place ^ 1 << stride) for place in range(count)]
    return lax.ppermute(block, "bfly", route)


def stacked(blocks):
    real, imag = blocks[:, 0], blocks[:, 1]
    top = jnp.concatenate([real, -imag], axis=-1)
    bottom = jnp.concatenate([imag, real], axis=-1)
    return jnp.concatenate([top, bottom], axis=-2)


def mul(matrix, values):
    return jnp.dot(matrix, values, preferred_element_type=jnp.float32)


def mul_t(matrix, values):
    contract = (((0,), (0,)), ((), ()))
    return lax.dot_general(matrix, values, contract, preferred_element_type=jnp.float32)


def turn(values, cosine, sine):
    rows = values.shape[0] // 2
    real, imag = values[:rows], values[rows:]
    return jnp.concatenate([cosine * real - sine * imag, sine * real + cosine * imag])


def turn_back(values, cosine, sine):
    rows = values.shape[0] // 2
    real, imag = values[:rows], values[rows:]
    return jnp.concatenate([cosine * real + sine * imag, cosine * imag - sine * real])


def row_dot(left, right):
    rows = left.shape[0] // 2
    product = left * right
    return jnp.sum(product[:rows] + product[rows:], axis=-1)


def local(sources, observed, receivers, model, phases, near_blocks, far_blocks, pattern):
    rows, columns = sources.shape[1:]
    levels = near_blocks.shape[0]
    rank = rows // pattern.shape[-1]
    repeats = columns // phases.shape[-1]
    bf16 = jnp.bfloat16

    sources = sources.reshape(2 * rows, columns)
    partner_sources = swapped(sources, 0)
    partner_model = swapped(model, 0)

    mask = jnp.repeat(jnp.repeat(pattern, rank, axis=2), rank, axis=3).astype(bf16)
    near = stacked(near_blocks * mask[:, 0:1])
    far = stacked(far_blocks * mask[:, 1:2])
    cosine = jnp.repeat(jnp.cos(phases), repeats, axis=-1)
    sine = jnp.repeat(jnp.sin(phases), repeats, axis=-1)

    selector = (receivers[:, None] == jnp.arange(rows, dtype=jnp.int32)[None, :]).astype(bf16)
    counts = jnp.sum(selector.astype(jnp.float32), axis=0)
    counts = jnp.concatenate([counts, counts])[:, None]
    spread = jnp.concatenate([mul_t(selector, observed[0]), mul_t(selector, observed[1])])
    data = turn_back(spread, cosine[-1], sine[-1])

    def start_field(values, factor):
        factor = jnp.concatenate([factor, factor])[:, None]
        return (factor * values.astype(jnp.float32)).astype(bf16)

    field = start_field(sources, model)
    partner_field = start_field(partner_sources, partner_model)
    for level in range(levels):
        if level:
            partner_field = swapped(field, level)
        mixed = mul(near[level], field) + mul(far[level], partner_field)
        if level < levels - 1:
            field = turn(mixed, cosine[level], sine[level]).astype(bf16)

    turned = (counts * mixed - data).astype(bf16)
    for level in reversed(range(1, levels)):
        far_term = swapped(mul_t(far[level], turned).astype(bf16), level)
        adjoint = mul_t(near[level], turned) + far_term.astype(jnp.float32)
        turned = turn_back(adjoint, cosine[level - 1], sine[level - 1]).astype(bf16)
    wide = sources.astype(jnp.float32)
    partial = row_dot(wide, mul_t(near[0], turned))
    partner_partial = row_dot(partner_sources.astype(jnp.float32), mul_t(far[0], turned))

    last = turn(mixed, cosine[-1], sine[-1]).astype(bf16)
    picked = jnp.stack([mul(selector, last[:rows]), mul(selector, last[rows:])])
    residual = picked - observed.astype(jnp.float32)

    illumination = row_dot(wide, wide)
    own = jnp.concatenate([partial, illumination])
    other = jnp.concatenate([partner_partial, jnp.zeros_like(illumination)])
    n_bfly, n_freq = lax.axis_size("bfly"), lax.axis_size("freq")
    first = lax.axis_index("bfly") % 2 == 0
    pair = jnp.stack([jnp.where(first, own, other), jnp.where(first, other, own)])
    terms = jnp.broadcast_to(pair[None], (n_freq, 2, 2 * rows)).reshape(2 * n_freq, 2 * rows)
    groups = [
        [f * n_bfly + high + low for f in range(n_freq) for low in range(2)]
        for high in range(0, n_bfly, 2)
    ]
    terms = lax.all_to_all(terms, ("freq", "bfly"), 0, 0, axis_index_groups=groups)
    total = jnp.sum(terms, axis=0)
    gradient = total[:rows] / jnp.sqrt(total[rows:] + epsilon)
    return (gradient, residual)


def solution(mesh):
    return jax.shard_map(
        local,
        mesh=mesh,
        in_specs=(
            P(None, "bfly", "freq"),
            P(None, "bfly", "freq"),
            P("bfly"),
            P("bfly"),
            P(None, "bfly", "freq"),
            P(None, None, "bfly", None),
            P(None, None, "bfly", None),
            P(None, None, "bfly", None),
        ),
        out_specs=(P("bfly"), P(None, "bfly", "freq")),
        check_vma=False,
    )
```

```python
import jax
import jax.numpy as jnp
from jax import lax
from jax.experimental import pallas as pl
from jax.experimental.pallas import tpu as pltpu
from jax.sharding import PartitionSpec as P

epsilon = 1e-05
bf16, f32 = jnp.bfloat16, jnp.float32
VMEM = pl.BlockSpec(memory_space=pltpu.VMEM)
SMEM = pl.BlockSpec(memory_space=pltpu.SMEM)


def swapped(block, stride):
    count = lax.axis_size("bfly")
    route = [(place, place ^ 1 << stride) for place in range(count)]
    return lax.ppermute(block, "bfly", route)


def after(values, *done):
    return lax.optimization_barrier((values, *done))[0]


def stacked(block):
    real, imag = block[0], block[1]
    top = jnp.concatenate([real, -imag], axis=-1)
    bottom = jnp.concatenate([imag, real], axis=-1)
    return jnp.concatenate([top, bottom], axis=-2)


def mul(matrix, values):
    return jnp.dot(matrix, values, preferred_element_type=f32)


def mul_t(matrix, values):
    contract = (((0,), (0,)), ((), ()))
    return lax.dot_general(matrix, values, contract, preferred_element_type=f32)


def turn(values, cosine, sine):
    rows = values.shape[0] // 2
    real, imag = values[:rows], values[rows:]
    return jnp.concatenate([cosine * real - sine * imag, sine * real + cosine * imag])


def turn_back(values, cosine, sine):
    rows = values.shape[0] // 2
    real, imag = values[:rows], values[rows:]
    return jnp.concatenate([cosine * real + sine * imag, cosine * imag - sine * real])


def masked(blocks, pattern_ref, level, kind):
    rows = blocks.shape[-1]
    half = rows // 2

    def band(side):
        keep = [
            jnp.broadcast_to(pattern_ref[kind, side, part : part + 1, level : level + 1], (half, half))
            for part in range(2)
        ]
        return jnp.concatenate(keep, axis=1).astype(f32).astype(bf16)

    mask = jnp.concatenate([band(0), band(1)])
    return [blocks[part] * mask for part in range(2)]


def waves(angles, columns):
    count = angles.shape[0]
    both = jnp.concatenate([jnp.cos(angles), jnp.sin(angles)])
    place = lax.broadcasted_iota(jnp.int32, (2 * count, 2 * columns), 1) // (columns // count)
    pick = (place == lax.broadcasted_iota(jnp.int32, place.shape, 0)).astype(f32)
    contract = (((0,), (0,)), ((), ()))
    return lax.dot_general(
        both, pick, contract, precision=lax.Precision.HIGHEST, preferred_element_type=f32
    )


def first_field(sources_ref, model_ref, field_out):
    rows = model_ref.shape[-1]
    place = lax.broadcasted_iota(jnp.int32, (rows, rows), 0)
    diagonal = place == lax.broadcasted_iota(jnp.int32, (rows, rows), 1)
    factor = jnp.sum(jnp.where(diagonal, model_ref[...], 0.0), axis=1, keepdims=True)
    for part in range(2):
        field = factor * sources_ref[part].astype(f32)
        field_out[part * rows : (part + 1) * rows] = field.astype(bf16)


def first_maps(near_ref, far_ref, pattern_ref, phases_ref, near_out, far_out, waves_out):
    near_out[...] = stacked(masked(near_ref[0], pattern_ref, 0, 0))
    far_out[...] = stacked(masked(far_ref[0], pattern_ref, 0, 1))
    waves_out[...] = waves(phases_ref[0], waves_out.shape[-1] // 2)


def later_maps(
    near_ref, far_ref, pattern_ref, phases_ref, observed_ref, receivers_ref,
    near_out, far_out, waves_out, select_out, counts_out, data_out,
):
    rows, columns = observed_ref.shape[1:]
    for level in range(1, 4):
        near_out[level - 1] = stacked(masked(near_ref[level], pattern_ref, level, 0))
        far_out[level - 1] = stacked(masked(far_ref[level], pattern_ref, level, 1))
        waves_out[level - 1] = waves(phases_ref[level], columns)
    select = receivers_ref[...] == lax.broadcasted_iota(jnp.int32, (rows, rows), 0)
    select = select.astype(f32)
    counts = jnp.broadcast_to(jnp.sum(select, axis=1, keepdims=True), (rows, columns))
    counts_out[...] = jnp.concatenate([counts, counts])
    select = select.astype(bf16)
    select_out[...] = select
    spread = jnp.concatenate([mul(select, observed_ref[0]), mul(select, observed_ref[1])])
    cosine, sine = waves_out[2, :, :columns], waves_out[2, :, columns:]
    data_out[...] = turn_back(spread, cosine, sine)


def last_terms(turned_ref, near_ref, far_ref, sources_ref, partner_ref, first_ref, terms_out):
    rows = sources_ref.shape[0] // 2
    wide = sources_ref[...].astype(f32)
    partner = partner_ref[...].astype(f32)
    turned = turned_ref[...]

    def row_sums(product):
        total = product[:rows] + product[rows:]
        return jnp.sum(total.T, axis=0, keepdims=True)

    own = row_sums(wide * mul_t(near_ref[...], turned))
    other = row_sums(partner * mul_t(far_ref[...], turned))
    own = jnp.concatenate([own, row_sums(wide * wide)], axis=1)
    other = jnp.concatenate([other, jnp.zeros_like(other)], axis=1)
    first = first_ref[0] == 0
    even, odd = jnp.where(first, own, other), jnp.where(first, other, own)
    n_freq = terms_out.shape[0] // 2
    pair = jnp.concatenate([even, odd])
    terms_out[...] = jnp.concatenate([pair[None]] * n_freq).reshape(terms_out.shape)


def local(sources, observed, receivers, model, phases, near_blocks, far_blocks, pattern):
    rows, columns = sources.shape[1:]
    shape = pltpu.VMEM
    phases = phases.transpose(0, 2, 1)
    pattern = pattern.transpose(1, 2, 3, 0)

    field = pl.pallas_call(
        first_field,
        out_shape=shape((2 * rows, columns), bf16),
        in_specs=[VMEM, VMEM],
        out_specs=VMEM,
        name="first_field",
    )(sources, model[None])
    partner = swapped(field, 0)
    blocks = pl.BlockSpec((1, 2, rows, rows), lambda step: (0, 0, 0, 0))
    angles = pl.BlockSpec((1, *phases.shape[1:]), lambda step: (0, 0, 0))
    near_0, far_0, waves_0 = pl.pallas_call(
        first_maps,
        out_shape=(
            shape((2 * rows, 2 * rows), bf16),
            shape((2 * rows, 2 * rows), bf16),
            shape((rows, 2 * columns), f32),
        ),
        grid=(1,),
        in_specs=[blocks, blocks, VMEM, angles],
        out_specs=(VMEM,) * 3,
        name="first_maps",
    )(near_blocks, far_blocks, pattern, phases)
    cosine_0, sine_0 = waves_0[:, :columns], waves_0[:, columns:]
    mixed = mul(near_0, field) + mul(far_0, partner)
    field = turn(mixed, cosine_0, sine_0).astype(bf16)

    partner = swapped(field, 1)
    near, far, wave, select, counts, data = pl.pallas_call(
        later_maps,
        out_shape=(
            shape((3, 2 * rows, 2 * rows), bf16),
            shape((3, 2 * rows, 2 * rows), bf16),
            shape((3, rows, 2 * columns), f32),
            shape((rows, rows), bf16),
            shape((2 * rows, columns), f32),
            shape((2 * rows, columns), f32),
        ),
        in_specs=[VMEM] * 6,
        out_specs=(VMEM,) * 6,
        name="later_maps",
    )(near_blocks, far_blocks, pattern, phases, observed, after(receivers, field)[None])
    near_1, near_2, near_3 = near
    far_1, far_2, far_3 = far
    (cosine_1, sine_1), (cosine_2, sine_2), (cosine_3, sine_3) = (
        (each[:, :columns], each[:, columns:]) for each in wave
    )
    mixed = mul(near_1, field) + mul(far_1, partner)
    field = turn(mixed, cosine_1, sine_1).astype(bf16)

    partner = swapped(field, 2)
    mixed = mul(near_2, field) + mul(far_2, partner)
    field = turn(mixed, cosine_2, sine_2).astype(bf16)

    partner = swapped(field, 3)
    sources = sources.reshape(2 * rows, columns)
    partner_sources = swapped(after(sources, field), 0)
    mixed = mul(near_3, field) + mul(far_3, partner)
    turned = (counts * mixed - data).astype(bf16)

    far_term = swapped(mul_t(far_3, turned).astype(bf16), 3)
    last = turn(mixed, cosine_3, sine_3).astype(bf16)
    picked = jnp.stack([mul_t(select, last[:rows]), mul_t(select, last[rows:])])
    residual = picked - observed.astype(f32)
    adjoint = mul_t(near_3, turned) + far_term.astype(f32)
    turned = turn_back(adjoint, cosine_2, sine_2).astype(bf16)

    far_term = swapped(mul_t(far_2, turned).astype(bf16), 2)
    adjoint = mul_t(near_2, turned) + far_term.astype(f32)
    turned = turn_back(adjoint, cosine_1, sine_1).astype(bf16)

    far_term = swapped(mul_t(far_1, turned).astype(bf16), 1)
    adjoint = mul_t(near_1, turned) + far_term.astype(f32)
    turned = turn_back(adjoint, cosine_0, sine_0).astype(bf16)

    n_bfly, n_freq = lax.axis_size("bfly"), lax.axis_size("freq")
    terms = pl.pallas_call(
        last_terms,
        out_shape=jax.ShapeDtypeStruct((2 * n_freq, 1, 2 * rows), f32),
        in_specs=[VMEM] * 5 + [SMEM],
        out_specs=VMEM,
        name="last_terms",
    )(
        *(
            pltpu.with_memory_space_constraint(each, pltpu.VMEM)
            for each in (turned, near_0, far_0, sources, partner_sources)
        ),
        (lax.axis_index("bfly") & 1)[None],
    )
    groups = [
        [f * n_bfly + high + low for f in range(n_freq) for low in range(2)]
        for high in range(0, n_bfly, 2)
    ]
    terms = lax.all_to_all(terms, ("freq", "bfly"), 0, 0, axis_index_groups=groups)
    total = jnp.sum(terms, axis=(0, 1))
    gradient = total[:rows] / jnp.sqrt(total[rows:] + epsilon)
    return (gradient, residual)


def solution(mesh):
    return jax.shard_map(
        local,
        mesh=mesh,
        in_specs=(
            P(None, "bfly", "freq"),
            P(None, "bfly", "freq"),
            P("bfly"),
            P("bfly"),
            P(None, "bfly", "freq"),
            P(None, None, "bfly", None),
            P(None, None, "bfly", None),
            P(None, None, "bfly", None),
        ),
        out_specs=(P("bfly"), P(None, "bfly", "freq")),
        check_vma=False,
    )
```

```python
import jax
import jax.numpy as jnp
from jax import lax
from jax.experimental import pallas as pl
from jax.experimental.pallas import tpu as pltpu
from jax.sharding import PartitionSpec as P

epsilon = 1e-05
bf16, f32 = jnp.bfloat16, jnp.float32
VMEM = pl.BlockSpec(memory_space=pltpu.VMEM)
SMEM = pl.BlockSpec(memory_space=pltpu.SMEM)


def swapped(block, stride):
    count = lax.axis_size("bfly")
    route = [(place, place ^ 1 << stride) for place in range(count)]
    return lax.ppermute(block, "bfly", route)


def after(values, *done):
    return lax.optimization_barrier((values, *done))[0]


def stacked(block):
    real, imag = block[0], block[1]
    top = jnp.concatenate([real, -imag], axis=-1)
    bottom = jnp.concatenate([imag, real], axis=-1)
    return jnp.concatenate([top, bottom], axis=-2)


def mul(matrix, values):
    return jnp.dot(matrix, values, preferred_element_type=f32)


def mul_t(matrix, values):
    contract = (((0,), (0,)), ((), ()))
    return lax.dot_general(matrix, values, contract, preferred_element_type=f32)


def turn(values, cosine, sine):
    rows = values.shape[0] // 2
    real, imag = values[:rows], values[rows:]
    return jnp.concatenate([cosine * real - sine * imag, sine * real + cosine * imag])


def turn_back(values, cosine, sine):
    rows = values.shape[0] // 2
    real, imag = values[:rows], values[rows:]
    return jnp.concatenate([cosine * real + sine * imag, cosine * imag - sine * real])


def masked(blocks, pattern_ref, level, kind):
    rows = blocks.shape[-1]
    half = rows // 2

    def band(side):
        keep = [
            jnp.broadcast_to(pattern_ref[kind, side, part : part + 1, level : level + 1], (half, half))
            for part in range(2)
        ]
        return jnp.concatenate(keep, axis=1).astype(f32).astype(bf16)

    mask = jnp.concatenate([band(0), band(1)])
    return [blocks[part] * mask for part in range(2)]


def waves(angles, columns):
    count = angles.shape[0]
    both = jnp.concatenate([jnp.cos(angles), jnp.sin(angles)])
    place = lax.broadcasted_iota(jnp.int32, (2 * count, 2 * columns), 1) // (columns // count)
    pick = (place == lax.broadcasted_iota(jnp.int32, place.shape, 0)).astype(f32)
    contract = (((0,), (0,)), ((), ()))
    return lax.dot_general(
        both, pick, contract, precision=lax.Precision.HIGHEST, preferred_element_type=f32
    )


def first_field(sources_ref, model_ref, field_out):
    rows = model_ref.shape[-1]
    place = lax.broadcasted_iota(jnp.int32, (rows, rows), 0)
    diagonal = place == lax.broadcasted_iota(jnp.int32, (rows, rows), 1)
    factor = jnp.sum(jnp.where(diagonal, model_ref[...], 0.0), axis=1, keepdims=True)
    for part in range(2):
        field = factor * sources_ref[part].astype(f32)
        field_out[part * rows : (part + 1) * rows] = field.astype(bf16)


def first_maps(
    sources_ref, near_ref, far_ref, pattern_ref, phases_ref, near_out, far_out, waves_out, lend_out
):
    rows, columns = sources_ref.shape[1:]
    near = masked(near_ref[0], pattern_ref, 0, 0)
    far = masked(far_ref[0], pattern_ref, 0, 1)
    near_out[...] = stacked(near)
    far_out[...] = stacked(far)
    angles = phases_ref[0]
    waves_out[...] = waves(angles, columns)
    for part in range(2):
        lend_out[part * rows : (part + 1) * rows] = sources_ref[part]
        both = jnp.concatenate([near[part], far[part]], axis=1)
        lend_out[(2 + part) * rows : (3 + part) * rows] = both
    high = angles.astype(bf16).astype(f32)
    middle = (angles - high).astype(bf16).astype(f32)
    low = angles - high - middle
    low = jnp.concatenate([low, jnp.zeros_like(low)], axis=1)
    split = jnp.concatenate([jnp.concatenate([high, middle], axis=1), low])
    lend_out[4 * rows :] = jnp.concatenate([split, jnp.zeros_like(split)]).astype(bf16)


def lent_maps(lent_ref, near_out, far_out, waves_out):
    columns = lent_ref.shape[1]
    rows = near_out.shape[0] // 2
    split = lent_ref[4 * rows :].astype(f32)
    count = split.shape[0] // 4
    angles = split[:count, :rows] + split[:count, rows:] + split[count : 2 * count, :rows]
    waves_out[...] = waves(angles, columns)
    real, imag = lent_ref[2 * rows : 3 * rows], lent_ref[3 * rows : 4 * rows]
    near_out[...] = stacked([real[:, :rows], imag[:, :rows]])
    far_out[...] = stacked([real[:, rows:], imag[:, rows:]])


def later_maps(
    near_ref, far_ref, pattern_ref, phases_ref, observed_ref, receivers_ref,
    near_out, far_out, waves_out, select_out, counts_out, data_out,
):
    rows, columns = observed_ref.shape[1:]
    for level in range(1, 4):
        near_out[level - 1] = stacked(masked(near_ref[level], pattern_ref, level, 0))
        far_out[level - 1] = stacked(masked(far_ref[level], pattern_ref, level, 1))
        waves_out[level - 1] = waves(phases_ref[level], columns)
    select = receivers_ref[...] == lax.broadcasted_iota(jnp.int32, (rows, rows), 0)
    select = select.astype(f32)
    counts = jnp.broadcast_to(jnp.sum(select, axis=1, keepdims=True), (rows, columns))
    counts_out[...] = jnp.concatenate([counts, counts])
    select = select.astype(bf16)
    select_out[...] = select
    spread = jnp.concatenate([mul(select, observed_ref[0]), mul(select, observed_ref[1])])
    cosine, sine = waves_out[2, :, :columns], waves_out[2, :, columns:]
    data_out[...] = turn_back(spread, cosine, sine)


def last_terms(
    turned_ref, near_1_ref, far_1_ref, near_ref, far_ref, waves_ref, near_2_ref, far_2_ref,
    waves_2_ref, sources_ref, lent_ref, across_ref, place_ref, terms_out,
):
    rows = sources_ref.shape[0] // 2
    columns = sources_ref.shape[1]

    def row_sums(product):
        total = product[:rows] + product[rows:]
        return jnp.sum(total.T, axis=0, keepdims=True)

    def term(sources, maps_ref, turned):
        return row_sums(sources.astype(f32) * mul_t(maps_ref[...], turned))

    def turned_by(values, wave_ref):
        return turn_back(values, wave_ref[:, :columns], wave_ref[:, columns:]).astype(bf16)

    turned = turned_ref[...]
    own = turned_by(mul_t(near_1_ref[...], turned), waves_ref)
    other = turned_by(mul_t(far_1_ref[...], turned), waves_2_ref)
    terms = [
        term(sources_ref[...], near_ref, own),
        term(across_ref[: 2 * rows], far_ref, own),
        term(lent_ref[: 2 * rows], near_2_ref, other),
        term(across_ref[2 * rows :], far_2_ref, other),
    ]
    wide = sources_ref[...].astype(f32)
    light = row_sums(wide * wide)
    lights = [light] + [jnp.zeros_like(light)] * 3
    terms = [jnp.concatenate(pair, axis=1) for pair in zip(terms, lights)]
    for bit in (1, 2):
        swap = place_ref[0] & bit != 0
        terms = [jnp.where(swap, terms[n ^ bit], terms[n]) for n in range(4)]
    quad = jnp.concatenate(terms)
    n_freq = terms_out.shape[0] // 4
    terms_out[...] = jnp.concatenate([quad[None]] * n_freq).reshape(terms_out.shape)


def in_hbm(values):
    return pltpu.with_memory_space_constraint(values, pltpu.HBM)


def in_vmem(values):
    return pltpu.with_memory_space_constraint(values, pltpu.VMEM)


def local(sources, observed, receivers, model, phases, near_blocks, far_blocks, pattern):
    rows, columns = sources.shape[1:]
    shape = pltpu.VMEM
    phases = phases.transpose(0, 2, 1)
    pattern = pattern.transpose(1, 2, 3, 0)

    field = pl.pallas_call(
        first_field,
        out_shape=shape((2 * rows, columns), bf16),
        in_specs=[VMEM, VMEM],
        out_specs=VMEM,
        compiler_params=pltpu.CompilerParams(vmem_limit_bytes=16 << 20),
        name="first_field",
    )(in_hbm(sources), in_hbm(model[None]))
    partner = swapped(field, 0)
    blocks = pl.BlockSpec((1, 2, rows, rows), lambda step: (0, 0, 0, 0))
    angles = pl.BlockSpec((1, *phases.shape[1:]), lambda step: (0, 0, 0))
    near_0, far_0, waves_0, lend = pl.pallas_call(
        first_maps,
        out_shape=(
            shape((2 * rows, 2 * rows), bf16),
            shape((2 * rows, 2 * rows), bf16),
            shape((rows, 2 * columns), f32),
            shape((4 * rows + 16, columns), bf16),
        ),
        grid=(1,),
        in_specs=[VMEM, blocks, blocks, VMEM, angles],
        out_specs=(VMEM,) * 4,
        compiler_params=pltpu.CompilerParams(vmem_limit_bytes=16 << 20),
        name="first_maps",
    )(*map(in_hbm, (sources, near_blocks, far_blocks, pattern, phases)))
    cosine_0, sine_0 = waves_0[:, :columns], waves_0[:, columns:]
    mixed = mul(near_0, field) + mul(far_0, partner)
    field = turn(mixed, cosine_0, sine_0).astype(bf16)

    partner = swapped(field, 1)
    lent = swapped(after(lend, field), 1)
    near, far, wave, select, counts, data = pl.pallas_call(
        later_maps,
        out_shape=(
            shape((3, 2 * rows, 2 * rows), bf16),
            shape((3, 2 * rows, 2 * rows), bf16),
            shape((3, rows, 2 * columns), f32),
            shape((rows, rows), bf16),
            shape((2 * rows, columns), f32),
            shape((2 * rows, columns), f32),
        ),
        in_specs=[VMEM] * 6,
        out_specs=(VMEM,) * 6,
        compiler_params=pltpu.CompilerParams(vmem_limit_bytes=16 << 20),
        name="later_maps",
    )(*map(in_hbm, (near_blocks, far_blocks, pattern, phases, observed)), after(receivers, field)[None])
    near_1, near_2, near_3 = near
    far_1, far_2, far_3 = far
    (cosine_1, sine_1), (cosine_2, sine_2), (cosine_3, sine_3) = (
        (each[:, :columns], each[:, columns:]) for each in wave
    )
    mixed = mul(near_1, field) + mul(far_1, partner)
    field = turn(mixed, cosine_1, sine_1).astype(bf16)

    partner = swapped(field, 2)
    mixed = mul(near_2, field) + mul(far_2, partner)
    field = turn(mixed, cosine_2, sine_2).astype(bf16)

    partner = swapped(field, 3)
    sources = sources.reshape(2 * rows, columns)
    lent = after(lent, field)
    across = swapped(jnp.concatenate([sources, lent[: 2 * rows]]), 0)
    near_lent, far_lent, waves_lent = pl.pallas_call(
        lent_maps,
        out_shape=(
            shape((2 * rows, 2 * rows), bf16),
            shape((2 * rows, 2 * rows), bf16),
            shape((rows, 2 * columns), f32),
        ),
        in_specs=[VMEM],
        out_specs=(VMEM,) * 3,
        compiler_params=pltpu.CompilerParams(vmem_limit_bytes=16 << 20),
        name="lent_maps",
    )(in_vmem(lent))
    mixed = mul(near_3, field) + mul(far_3, partner)
    turned = (counts * mixed - data).astype(bf16)

    far_term = swapped(mul_t(far_3, turned).astype(bf16), 3)
    last = turn(mixed, cosine_3, sine_3).astype(bf16)
    picked = jnp.stack([mul_t(select, last[:rows]), mul_t(select, last[rows:])])
    residual = picked - observed.astype(f32)
    adjoint = lax.optimization_barrier(mul_t(near_3, turned)) + far_term.astype(f32)
    turned = turn_back(adjoint, cosine_2, sine_2).astype(bf16)

    far_term = swapped(mul_t(far_2, turned).astype(bf16), 2)
    adjoint = lax.optimization_barrier(mul_t(near_2, turned)) + far_term.astype(f32)
    turned = turn_back(adjoint, cosine_1, sine_1).astype(bf16)

    n_bfly, n_freq = lax.axis_size("bfly"), lax.axis_size("freq")
    inputs = (turned, near_1, far_1, near_0, far_0, waves_0, near_lent, far_lent, waves_lent)
    terms = pl.pallas_call(
        last_terms,
        out_shape=jax.ShapeDtypeStruct((4 * n_freq, 1, 2 * rows), f32),
        in_specs=[VMEM] * 12 + [SMEM],
        out_specs=VMEM,
        compiler_params=pltpu.CompilerParams(vmem_limit_bytes=16 << 20),
        name="last_terms",
    )(*map(in_vmem, (*inputs, sources, lent, across)), (lax.axis_index("bfly") & 3)[None])
    groups = [
        [f * n_bfly + high + low for f in range(n_freq) for low in range(4)]
        for high in range(0, n_bfly, 4)
    ]
    terms = lax.all_to_all(terms, ("freq", "bfly"), 0, 0, axis_index_groups=groups)
    total = jnp.sum(terms, axis=(0, 1))
    gradient = total[:rows] / jnp.sqrt(total[rows:] + epsilon)
    return (gradient, residual)


def solution(mesh):
    return jax.shard_map(
        local,
        mesh=mesh,
        in_specs=(
            P(None, "bfly", "freq"),
            P(None, "bfly", "freq"),
            P("bfly"),
            P("bfly"),
            P(None, "bfly", "freq"),
            P(None, None, "bfly", None),
            P(None, None, "bfly", None),
            P(None, None, "bfly", None),
        ),
        out_specs=(P("bfly"), P(None, "bfly", "freq")),
        check_vma=False,
    )
```

```python
import jax
import jax.numpy as jnp
from jax import lax
from jax.experimental import pallas as pl
from jax.experimental.pallas import tpu as pltpu
from jax.sharding import PartitionSpec as P

epsilon = 1e-05
bf16, f32 = jnp.bfloat16, jnp.float32
VMEM = pl.BlockSpec(memory_space=pltpu.VMEM)
SMEM = pl.BlockSpec(memory_space=pltpu.SMEM)


def swapped(block, stride):
    count = lax.axis_size("bfly")
    route = [(place, place ^ 1 << stride) for place in range(count)]
    return lax.ppermute(block, "bfly", route)


def traded(block, stride):
    count = lax.axis_size("bfly")
    pairs = [[low, low | 1 << stride] for low in range(count) if not low >> stride & 1]
    both = lax.all_gather(block, "bfly", axis_index_groups=pairs)
    return jnp.where((lax.axis_index("bfly") >> stride & 1) == 0, both[1], both[0])


def after(values, *done):
    return lax.optimization_barrier((values, *done))[0]


def stacked(block):
    real, imag = block[0], block[1]
    top = jnp.concatenate([real, -imag], axis=-1)
    bottom = jnp.concatenate([imag, real], axis=-1)
    return jnp.concatenate([top, bottom], axis=-2)


def mul(matrix, values):
    return jnp.dot(matrix, values, preferred_element_type=f32)


def mul_t(matrix, values):
    contract = (((0,), (0,)), ((), ()))
    return lax.dot_general(matrix, values, contract, preferred_element_type=f32)


def turn(values, cosine, sine):
    rows = values.shape[0] // 2
    real, imag = values[:rows], values[rows:]
    return jnp.concatenate([cosine * real - sine * imag, sine * real + cosine * imag])


def turn_back(values, cosine, sine):
    rows = values.shape[0] // 2
    real, imag = values[:rows], values[rows:]
    return jnp.concatenate([cosine * real + sine * imag, cosine * imag - sine * real])


def masked(blocks, pattern_ref, level, kind):
    rows = blocks.shape[-1]
    half = rows // 2

    def band(side):
        keep = [
            jnp.broadcast_to(pattern_ref[kind, side, part : part + 1, level : level + 1], (half, half))
            for part in range(2)
        ]
        return jnp.concatenate(keep, axis=1).astype(f32).astype(bf16)

    mask = jnp.concatenate([band(0), band(1)])
    return [blocks[part] * mask for part in range(2)]


def waves(angles, columns):
    count = angles.shape[0]
    both = jnp.concatenate([jnp.cos(angles), jnp.sin(angles)])
    place = lax.broadcasted_iota(jnp.int32, (2 * count, 2 * columns), 1) // (columns // count)
    pick = (place == lax.broadcasted_iota(jnp.int32, place.shape, 0)).astype(f32)
    contract = (((0,), (0,)), ((), ()))
    return lax.dot_general(
        both, pick, contract, precision=lax.Precision.HIGHEST, preferred_element_type=f32
    )


def first_field(sources_ref, model_ref, field_out):
    rows = model_ref.shape[-1]
    place = lax.broadcasted_iota(jnp.int32, (rows, rows), 0)
    diagonal = place == lax.broadcasted_iota(jnp.int32, (rows, rows), 1)
    factor = jnp.sum(jnp.where(diagonal, model_ref[...], 0.0), axis=1, keepdims=True)
    for part in range(2):
        field = factor * sources_ref[part].astype(f32)
        field_out[part * rows : (part + 1) * rows] = field.astype(bf16)


def first_maps(
    sources_ref, near_ref, far_ref, pattern_ref, phases_ref, near_out, far_out, waves_out, lend_out
):
    rows, columns = sources_ref.shape[1:]
    near = masked(near_ref[0], pattern_ref, 0, 0)
    far = masked(far_ref[0], pattern_ref, 0, 1)
    near_out[...] = stacked(near)
    far_out[...] = stacked(far)
    angles = phases_ref[0]
    waves_out[...] = waves(angles, columns)
    for part in range(2):
        lend_out[part * rows : (part + 1) * rows] = sources_ref[part]
        both = jnp.concatenate([near[part], far[part]], axis=1)
        lend_out[(2 + part) * rows : (3 + part) * rows] = both
    high = angles.astype(bf16).astype(f32)
    middle = (angles - high).astype(bf16).astype(f32)
    low = angles - high - middle
    low = jnp.concatenate([low, jnp.zeros_like(low)], axis=1)
    split = jnp.concatenate([jnp.concatenate([high, middle], axis=1), low])
    lend_out[4 * rows :] = jnp.concatenate([split, jnp.zeros_like(split)]).astype(bf16)


def lent_maps(lent_ref, near_out, far_out, waves_out):
    columns = lent_ref.shape[1]
    rows = near_out.shape[0] // 2
    split = lent_ref[4 * rows :].astype(f32)
    count = split.shape[0] // 4
    angles = split[:count, :rows] + split[:count, rows:] + split[count : 2 * count, :rows]
    waves_out[...] = waves(angles, columns)
    real, imag = lent_ref[2 * rows : 3 * rows], lent_ref[3 * rows : 4 * rows]
    near_out[...] = stacked([real[:, :rows], imag[:, :rows]])
    far_out[...] = stacked([real[:, rows:], imag[:, rows:]])


def middle_maps(near_ref, far_ref, pattern_ref, phases_ref, near_out, far_out, waves_out):
    near_out[...] = stacked(masked(near_ref[0], pattern_ref, 1, 0))
    far_out[...] = stacked(masked(far_ref[0], pattern_ref, 1, 1))
    waves_out[...] = waves(phases_ref[0], waves_out.shape[-1] // 2)


def later_maps(
    near_ref, far_ref, pattern_ref, phases_ref, observed_ref, receivers_ref,
    near_out, far_out, waves_out, select_out, counts_out, data_out,
):
    rows, columns = observed_ref.shape[1:]
    for level in range(2, 4):
        near_out[level - 2] = stacked(masked(near_ref[level - 2], pattern_ref, level, 0))
        far_out[level - 2] = stacked(masked(far_ref[level - 2], pattern_ref, level, 1))
        waves_out[level - 2] = waves(phases_ref[level - 2], columns)
    select = receivers_ref[...] == lax.broadcasted_iota(jnp.int32, (rows, rows), 0)
    select = select.astype(f32)
    counts = jnp.broadcast_to(jnp.sum(select, axis=1, keepdims=True), (rows, columns))
    counts_out[...] = jnp.concatenate([counts, counts])
    select = select.astype(bf16)
    select_out[...] = select
    spread = jnp.concatenate([mul(select, observed_ref[0]), mul(select, observed_ref[1])])
    cosine, sine = waves_out[1, :, :columns], waves_out[1, :, columns:]
    data_out[...] = turn_back(spread, cosine, sine)


def last_terms(
    turned_ref, near_1_ref, far_1_ref, near_ref, far_ref, waves_ref, near_2_ref, far_2_ref,
    waves_2_ref, sources_ref, lent_ref, across_ref, across_lent_ref, place_ref, terms_out,
):
    rows = sources_ref.shape[0] // 2
    columns = sources_ref.shape[1]

    def row_sums(product):
        total = product[:rows] + product[rows:]
        return jnp.sum(total.T, axis=0, keepdims=True)

    def term(sources, maps_ref, turned):
        return row_sums(sources.astype(f32) * mul_t(maps_ref[...], turned))

    def turned_by(values, wave_ref):
        return turn_back(values, wave_ref[:, :columns], wave_ref[:, columns:]).astype(bf16)

    turned = turned_ref[...]
    own = turned_by(mul_t(near_1_ref[...], turned), waves_ref)
    other = turned_by(mul_t(far_1_ref[...], turned), waves_2_ref)
    terms = [
        term(sources_ref[...], near_ref, own),
        term(across_ref[...], far_ref, own),
        term(lent_ref[: 2 * rows], near_2_ref, other),
        term(across_lent_ref[...], far_2_ref, other),
    ]
    wide = sources_ref[...].astype(f32)
    light = row_sums(wide * wide)
    lights = [light] + [jnp.zeros_like(light)] * 3
    terms = [jnp.concatenate(pair, axis=1) for pair in zip(terms, lights)]
    for bit in (1, 2):
        swap = place_ref[0] & bit != 0
        terms = [jnp.where(swap, terms[n ^ bit], terms[n]) for n in range(4)]
    quad = jnp.concatenate(terms)
    n_freq = terms_out.shape[0] // 4
    terms_out[...] = jnp.concatenate([quad[None]] * n_freq).reshape(terms_out.shape)


def last_ratio(terms_ref, gradient_out):
    rows = gradient_out.shape[-1]
    total = jnp.sum(terms_ref[...], axis=0)
    gradient_out[...] = total[:, :rows] / jnp.sqrt(total[:, rows:] + epsilon)


def in_hbm(values):
    return pltpu.with_memory_space_constraint(values, pltpu.HBM)


def in_vmem(values):
    return pltpu.with_memory_space_constraint(values, pltpu.VMEM)


def local(sources, observed, receivers, model, phases, near_blocks, far_blocks, pattern):
    rows, columns = sources.shape[1:]
    shape = pltpu.VMEM
    phases = phases.transpose(0, 2, 1)
    pattern = pattern.transpose(1, 2, 3, 0)

    field = pl.pallas_call(
        first_field,
        out_shape=shape((2 * rows, columns), bf16),
        in_specs=[VMEM, VMEM],
        out_specs=VMEM,
        compiler_params=pltpu.CompilerParams(vmem_limit_bytes=16 << 20),
        name="first_field",
    )(in_hbm(sources), in_hbm(model[None]))
    partner = swapped(field, 0)
    blocks = pl.BlockSpec((1, 2, rows, rows), lambda step: (0, 0, 0, 0))
    angles = pl.BlockSpec((1, *phases.shape[1:]), lambda step: (0, 0, 0))
    near_0, far_0, waves_0, lend = pl.pallas_call(
        first_maps,
        out_shape=(
            shape((2 * rows, 2 * rows), bf16),
            shape((2 * rows, 2 * rows), bf16),
            shape((rows, 2 * columns), f32),
            shape((4 * rows + 16, columns), bf16),
        ),
        grid=(1,),
        in_specs=[VMEM, blocks, blocks, VMEM, angles],
        out_specs=(VMEM,) * 4,
        compiler_params=pltpu.CompilerParams(vmem_limit_bytes=16 << 20),
        name="first_maps",
    )(*map(in_hbm, (sources, near_blocks, far_blocks, pattern, phases)))
    cosine_0, sine_0 = waves_0[:, :columns], waves_0[:, columns:]
    mixed = mul(near_0, field) + mul(far_0, partner)
    field = turn(mixed, cosine_0, sine_0).astype(bf16)

    partner = swapped(field, 1)
    lent = swapped(after(lend, field), 1)
    blocks = pl.BlockSpec((1, 2, rows, rows), lambda step: (1, 0, 0, 0))
    angles = pl.BlockSpec((1, *phases.shape[1:]), lambda step: (1, 0, 0))
    near_1, far_1, waves_1 = pl.pallas_call(
        middle_maps,
        out_shape=(
            shape((2 * rows, 2 * rows), bf16),
            shape((2 * rows, 2 * rows), bf16),
            shape((rows, 2 * columns), f32),
        ),
        grid=(1,),
        in_specs=[blocks, blocks, VMEM, angles],
        out_specs=(VMEM,) * 3,
        compiler_params=pltpu.CompilerParams(vmem_limit_bytes=16 << 20),
        name="middle_maps",
    )(*map(in_hbm, (near_blocks, far_blocks)), after(pattern, field), in_hbm(phases))
    cosine_1, sine_1 = waves_1[:, :columns], waves_1[:, columns:]
    mixed = mul(near_1, field) + mul(far_1, partner)
    field = turn(mixed, cosine_1, sine_1).astype(bf16)

    partner = swapped(field, 2)
    blocks = pl.BlockSpec((2, 2, rows, rows), lambda step: (1, 0, 0, 0))
    angles = pl.BlockSpec((2, *phases.shape[1:]), lambda step: (1, 0, 0))
    near, far, wave, select, counts, data = pl.pallas_call(
        later_maps,
        out_shape=(
            shape((2, 2 * rows, 2 * rows), bf16),
            shape((2, 2 * rows, 2 * rows), bf16),
            shape((2, rows, 2 * columns), f32),
            shape((rows, rows), bf16),
            shape((2 * rows, columns), f32),
            shape((2 * rows, columns), f32),
        ),
        grid=(1,),
        in_specs=[blocks, blocks, VMEM, angles, VMEM, VMEM],
        out_specs=(VMEM,) * 6,
        compiler_params=pltpu.CompilerParams(vmem_limit_bytes=16 << 20),
        name="later_maps",
    )(
        *map(in_hbm, (near_blocks, far_blocks, pattern, phases, observed)),
        after(receivers, field)[None],
    )
    near_2, near_3 = near
    far_2, far_3 = far
    (cosine_2, sine_2), (cosine_3, sine_3) = (
        (each[:, :columns], each[:, columns:]) for each in wave
    )
    mixed = mul(near_2, field) + mul(far_2, partner)
    field = turn(mixed, cosine_2, sine_2).astype(bf16)

    partner = swapped(field, 3)
    sources = sources.reshape(2 * rows, columns)
    lent = after(lent, field)
    across, across_lent = swapped(after(sources, field), 0), swapped(lent[: 2 * rows], 0)
    near_lent, far_lent, waves_lent = pl.pallas_call(
        lent_maps,
        out_shape=(
            shape((2 * rows, 2 * rows), bf16),
            shape((2 * rows, 2 * rows), bf16),
            shape((rows, 2 * columns), f32),
        ),
        in_specs=[VMEM],
        out_specs=(VMEM,) * 3,
        compiler_params=pltpu.CompilerParams(vmem_limit_bytes=16 << 20),
        name="lent_maps",
    )(in_vmem(lent))
    mixed = mul(near_3, field) + mul(far_3, partner)
    turned = (counts * mixed - data).astype(bf16)

    turned = after(turned, across, across_lent, near_lent)
    far_term = traded(mul_t(far_3, turned).astype(bf16), 3)
    last = turn(mixed, cosine_3, sine_3).astype(bf16)
    picked = jnp.stack([mul_t(select, last[:rows]), mul_t(select, last[rows:])])
    residual = picked - observed.astype(f32)
    adjoint = lax.optimization_barrier(mul_t(near_3, turned)) + far_term.astype(f32)
    turned = turn_back(adjoint, cosine_2, sine_2).astype(bf16)

    far_term = traded(mul_t(far_2, turned).astype(bf16), 2)
    adjoint = lax.optimization_barrier(mul_t(near_2, turned)) + far_term.astype(f32)
    turned = turn_back(adjoint, cosine_1, sine_1).astype(bf16)

    n_bfly, n_freq = lax.axis_size("bfly"), lax.axis_size("freq")
    inputs = (turned, near_1, far_1, near_0, far_0, waves_0, near_lent, far_lent, waves_lent)
    terms = pl.pallas_call(
        last_terms,
        out_shape=jax.ShapeDtypeStruct((4 * n_freq, 1, 2 * rows), f32),
        in_specs=[VMEM] * 13 + [SMEM],
        out_specs=VMEM,
        compiler_params=pltpu.CompilerParams(vmem_limit_bytes=16 << 20),
        name="last_terms",
    )(*map(in_vmem, (*inputs, sources, lent, across, across_lent)), (lax.axis_index("bfly") & 3)[None])
    groups = [
        [f * n_bfly + high + low for f in range(n_freq) for low in range(4)]
        for high in range(0, n_bfly, 4)
    ]
    terms = lax.all_to_all(terms, ("freq", "bfly"), 0, 0, axis_index_groups=groups)
    gradient = pl.pallas_call(
        last_ratio,
        out_shape=jax.ShapeDtypeStruct((1, rows), f32),
        in_specs=[VMEM],
        out_specs=VMEM,
        compiler_params=pltpu.CompilerParams(vmem_limit_bytes=16 << 20),
        name="last_ratio",
    )(in_vmem(terms))
    return (gradient[0], residual)


def solution(mesh):
    return jax.shard_map(
        local,
        mesh=mesh,
        in_specs=(
            P(None, "bfly", "freq"),
            P(None, "bfly", "freq"),
            P("bfly"),
            P("bfly"),
            P(None, "bfly", "freq"),
            P(None, None, "bfly", None),
            P(None, None, "bfly", None),
            P(None, None, "bfly", None),
        ),
        out_specs=(P("bfly"), P(None, "bfly", "freq")),
        check_vma=False,
    )
```

```python
import jax
import jax.numpy as jnp
from jax import lax
from jax.experimental import pallas as pl
from jax.experimental.pallas import tpu as pltpu
from jax.sharding import PartitionSpec as P

epsilon = 1e-05
bf16, f32 = jnp.bfloat16, jnp.float32
VMEM = pl.BlockSpec(memory_space=pltpu.VMEM)
SMEM = pl.BlockSpec(memory_space=pltpu.SMEM)


def swapped(block, stride):
    count = lax.axis_size("bfly")
    route = [(place, place ^ 1 << stride) for place in range(count)]
    return lax.ppermute(block, "bfly", route)


def traded(block, stride):
    count = lax.axis_size("bfly")
    pairs = [[low, low | 1 << stride] for low in range(count) if not low >> stride & 1]
    both = lax.all_gather(block, "bfly", axis_index_groups=pairs)
    return jnp.where((lax.axis_index("bfly") >> stride & 1) == 0, both[1], both[0])


def after(values, *done):
    return lax.optimization_barrier((values, *done))[0]


def stacked(block):
    real, imag = block[0], block[1]
    top = jnp.concatenate([real, -imag], axis=-1)
    bottom = jnp.concatenate([imag, real], axis=-1)
    return jnp.concatenate([top, bottom], axis=-2)


def mul(matrix, values):
    return jnp.dot(matrix, values, preferred_element_type=f32)


def mul_t(matrix, values):
    contract = (((0,), (0,)), ((), ()))
    return lax.dot_general(matrix, values, contract, preferred_element_type=f32)


def turn(values, cosine, sine):
    rows = values.shape[0] // 2
    real, imag = values[:rows], values[rows:]
    return jnp.concatenate([cosine * real - sine * imag, sine * real + cosine * imag])


def turn_back(values, cosine, sine):
    rows = values.shape[0] // 2
    real, imag = values[:rows], values[rows:]
    return jnp.concatenate([cosine * real + sine * imag, cosine * imag - sine * real])


def masked(blocks, pattern_ref, level, kind):
    rows = blocks.shape[-1]
    half = rows // 2

    def band(side):
        keep = [
            jnp.broadcast_to(pattern_ref[kind, side, part : part + 1, level : level + 1], (half, half))
            for part in range(2)
        ]
        return jnp.concatenate(keep, axis=1).astype(f32).astype(bf16)

    mask = jnp.concatenate([band(0), band(1)])
    return [blocks[part] * mask for part in range(2)]


def waves(angles, columns):
    count = angles.shape[0]
    both = jnp.concatenate([jnp.cos(angles), jnp.sin(angles)])
    place = lax.broadcasted_iota(jnp.int32, (2 * count, 2 * columns), 1) // (columns // count)
    pick = (place == lax.broadcasted_iota(jnp.int32, place.shape, 0)).astype(f32)
    contract = (((0,), (0,)), ((), ()))
    return lax.dot_general(
        both, pick, contract, precision=lax.Precision.HIGHEST, preferred_element_type=f32
    )


def first_field(sources_ref, model_ref, field_out):
    rows = model_ref.shape[-1]
    place = lax.broadcasted_iota(jnp.int32, (rows, rows), 0)
    diagonal = place == lax.broadcasted_iota(jnp.int32, (rows, rows), 1)
    factor = jnp.sum(jnp.where(diagonal, model_ref[...], 0.0), axis=1, keepdims=True)
    for part in range(2):
        field = factor * sources_ref[part].astype(f32)
        field_out[part * rows : (part + 1) * rows] = field.astype(bf16)


def first_maps(
    sources_ref, near_ref, far_ref, pattern_ref, phases_ref, near_out, far_out, waves_out, lend_out
):
    rows, columns = sources_ref.shape[1:]
    near = masked(near_ref[0], pattern_ref, 0, 0)
    far = masked(far_ref[0], pattern_ref, 0, 1)
    near_out[...] = stacked(near)
    far_out[...] = stacked(far)
    angles = phases_ref[0]
    waves_out[...] = waves(angles, columns)
    for part in range(2):
        lend_out[part * rows : (part + 1) * rows] = sources_ref[part]
        both = jnp.concatenate([near[part], far[part]], axis=1)
        lend_out[(2 + part) * rows : (3 + part) * rows] = both
    high = angles.astype(bf16).astype(f32)
    middle = (angles - high).astype(bf16).astype(f32)
    low = angles - high - middle
    low = jnp.concatenate([low, jnp.zeros_like(low)], axis=1)
    split = jnp.concatenate([jnp.concatenate([high, middle], axis=1), low])
    lend_out[4 * rows :] = jnp.concatenate([split, jnp.zeros_like(split)]).astype(bf16)


def lent_maps(lent_ref, near_out, far_out, waves_out):
    columns = lent_ref.shape[1]
    rows = near_out.shape[0] // 2
    split = lent_ref[4 * rows :].astype(f32)
    count = split.shape[0] // 4
    angles = split[:count, :rows] + split[:count, rows:] + split[count : 2 * count, :rows]
    waves_out[...] = waves(angles, columns)
    real, imag = lent_ref[2 * rows : 3 * rows], lent_ref[3 * rows : 4 * rows]
    near_out[...] = stacked([real[:, :rows], imag[:, :rows]])
    far_out[...] = stacked([real[:, rows:], imag[:, rows:]])


def middle_maps(near_ref, far_ref, pattern_ref, phases_ref, near_out, far_out, waves_out):
    near_out[...] = stacked(masked(near_ref[0], pattern_ref, 1, 0))
    far_out[...] = stacked(masked(far_ref[0], pattern_ref, 1, 1))
    waves_out[...] = waves(phases_ref[0], waves_out.shape[-1] // 2)


def later_maps(
    near_ref, far_ref, pattern_ref, phases_ref, observed_ref, receivers_ref,
    near_out, far_out, waves_out, select_out, counts_out, data_out,
):
    rows, columns = observed_ref.shape[1:]
    for level in range(2, 4):
        near_out[level - 2] = stacked(masked(near_ref[level - 2], pattern_ref, level, 0))
        far_out[level - 2] = stacked(masked(far_ref[level - 2], pattern_ref, level, 1))
        waves_out[level - 2] = waves(phases_ref[level - 2], columns)
    select = receivers_ref[...] == lax.broadcasted_iota(jnp.int32, (rows, rows), 0)
    select = select.astype(f32)
    counts = jnp.broadcast_to(jnp.sum(select, axis=1, keepdims=True), (rows, columns))
    counts_out[...] = jnp.concatenate([counts, counts])
    select = select.astype(bf16)
    select_out[...] = select
    spread = jnp.concatenate([mul(select, observed_ref[0]), mul(select, observed_ref[1])])
    cosine, sine = waves_out[1, :, :columns], waves_out[1, :, columns:]
    data_out[...] = turn_back(spread, cosine, sine)


def last_terms(
    turned_ref, near_1_ref, far_1_ref, near_ref, far_ref, waves_ref, near_2_ref, far_2_ref,
    waves_2_ref, sources_ref, lent_ref, across_ref, across_lent_ref, place_ref, terms_out,
):
    rows = sources_ref.shape[0] // 2
    columns = sources_ref.shape[1]

    def row_sums(product):
        total = product[:rows] + product[rows:]
        total = total[:, : columns // 2] + total[:, columns // 2 :]
        return jnp.sum(total.T, axis=0, keepdims=True)

    def term(sources, maps_ref, turned):
        return row_sums(sources.astype(f32) * mul_t(maps_ref[...], turned))

    def turned_by(values, wave_ref):
        return turn_back(values, wave_ref[:, :columns], wave_ref[:, columns:]).astype(bf16)

    turned = turned_ref[...]
    own = turned_by(mul_t(near_1_ref[...], turned), waves_ref)
    other = turned_by(mul_t(far_1_ref[...], turned), waves_2_ref)
    terms = [
        term(sources_ref[...], near_ref, own),
        term(across_ref[...], far_ref, own),
        term(lent_ref[: 2 * rows], near_2_ref, other),
        term(across_lent_ref[...], far_2_ref, other),
    ]
    wide = sources_ref[...].astype(f32)
    light = row_sums(wide * wide)
    lights = [light] + [jnp.zeros_like(light)] * 3
    terms = [jnp.concatenate(pair, axis=1) for pair in zip(terms, lights)]
    for bit in (1, 2):
        swap = place_ref[0] & bit != 0
        terms = [jnp.where(swap, terms[n ^ bit], terms[n]) for n in range(4)]
    quad = jnp.concatenate(terms)
    n_freq = terms_out.shape[0] // 4
    terms_out[...] = jnp.concatenate([quad[None]] * n_freq).reshape(terms_out.shape)


def last_ratio(terms_ref, gradient_out):
    rows = gradient_out.shape[-1]
    total = jnp.sum(terms_ref[...], axis=0)
    gradient_out[...] = total[:, :rows] / jnp.sqrt(total[:, rows:] + epsilon)


def in_hbm(values):
    return pltpu.with_memory_space_constraint(values, pltpu.HBM)


def in_vmem(values):
    return pltpu.with_memory_space_constraint(values, pltpu.VMEM)


def local(sources, observed, receivers, model, phases, near_blocks, far_blocks, pattern):
    rows, columns = sources.shape[1:]
    shape = pltpu.VMEM
    phases = phases.transpose(0, 2, 1)
    pattern = pattern.transpose(1, 2, 3, 0)

    field = pl.pallas_call(
        first_field,
        out_shape=shape((2 * rows, columns), bf16),
        in_specs=[VMEM, VMEM],
        out_specs=VMEM,
        compiler_params=pltpu.CompilerParams(vmem_limit_bytes=16 << 20),
        name="first_field",
    )(in_hbm(sources), in_hbm(model[None]))
    partner = swapped(field, 0)
    blocks = pl.BlockSpec((1, 2, rows, rows), lambda step: (0, 0, 0, 0))
    angles = pl.BlockSpec((1, *phases.shape[1:]), lambda step: (0, 0, 0))
    near_0, far_0, waves_0, lend = pl.pallas_call(
        first_maps,
        out_shape=(
            shape((2 * rows, 2 * rows), bf16),
            shape((2 * rows, 2 * rows), bf16),
            shape((rows, 2 * columns), f32),
            shape((4 * rows + 16, columns), bf16),
        ),
        grid=(1,),
        in_specs=[VMEM, blocks, blocks, VMEM, angles],
        out_specs=(VMEM,) * 4,
        compiler_params=pltpu.CompilerParams(vmem_limit_bytes=16 << 20),
        name="first_maps",
    )(*map(in_hbm, (sources, near_blocks, far_blocks, pattern, phases)))
    cosine_0, sine_0 = waves_0[:, :columns], waves_0[:, columns:]
    mixed = mul(near_0, field) + mul(far_0, partner)
    field = turn(mixed, cosine_0, sine_0).astype(bf16)

    partner = swapped(field, 1)
    lent = swapped(after(lend, field), 1)
    blocks = pl.BlockSpec((1, 2, rows, rows), lambda step: (1, 0, 0, 0))
    angles = pl.BlockSpec((1, *phases.shape[1:]), lambda step: (1, 0, 0))
    near_1, far_1, waves_1 = pl.pallas_call(
        middle_maps,
        out_shape=(
            shape((2 * rows, 2 * rows), bf16),
            shape((2 * rows, 2 * rows), bf16),
            shape((rows, 2 * columns), f32),
        ),
        grid=(1,),
        in_specs=[blocks, blocks, VMEM, angles],
        out_specs=(VMEM,) * 3,
        compiler_params=pltpu.CompilerParams(vmem_limit_bytes=16 << 20),
        name="middle_maps",
    )(*map(in_hbm, (near_blocks, far_blocks)), after(pattern, field), in_hbm(phases))
    cosine_1, sine_1 = waves_1[:, :columns], waves_1[:, columns:]
    mixed = mul(near_1, field) + mul(far_1, partner)
    field = turn(mixed, cosine_1, sine_1).astype(bf16)

    partner = swapped(field, 2)
    blocks = pl.BlockSpec((2, 2, rows, rows), lambda step: (1, 0, 0, 0))
    angles = pl.BlockSpec((2, *phases.shape[1:]), lambda step: (1, 0, 0))
    near, far, wave, select, counts, data = pl.pallas_call(
        later_maps,
        out_shape=(
            shape((2, 2 * rows, 2 * rows), bf16),
            shape((2, 2 * rows, 2 * rows), bf16),
            shape((2, rows, 2 * columns), f32),
            shape((rows, rows), bf16),
            shape((2 * rows, columns), f32),
            shape((2 * rows, columns), f32),
        ),
        grid=(1,),
        in_specs=[blocks, blocks, VMEM, angles, VMEM, VMEM],
        out_specs=(VMEM,) * 6,
        compiler_params=pltpu.CompilerParams(vmem_limit_bytes=16 << 20),
        name="later_maps",
    )(
        *map(in_hbm, (near_blocks, far_blocks, pattern, phases, observed)),
        after(receivers, field)[None],
    )
    near_2, near_3 = near
    far_2, far_3 = far
    (cosine_2, sine_2), (cosine_3, sine_3) = (
        (each[:, :columns], each[:, columns:]) for each in wave
    )
    mixed = mul(near_2, field) + mul(far_2, partner)
    field = turn(mixed, cosine_2, sine_2).astype(bf16)

    partner = swapped(field, 3)
    sources = sources.reshape(2 * rows, columns)
    lent = after(lent, field)
    across, across_lent = swapped(after(sources, field), 0), swapped(lent[: 2 * rows], 0)
    near_lent, far_lent, waves_lent = pl.pallas_call(
        lent_maps,
        out_shape=(
            shape((2 * rows, 2 * rows), bf16),
            shape((2 * rows, 2 * rows), bf16),
            shape((rows, 2 * columns), f32),
        ),
        in_specs=[VMEM],
        out_specs=(VMEM,) * 3,
        compiler_params=pltpu.CompilerParams(vmem_limit_bytes=16 << 20),
        name="lent_maps",
    )(in_vmem(lent))
    mixed = mul(near_3, field) + mul(far_3, partner)
    turned = (counts * mixed - data).astype(bf16)

    turned = after(turned, across, across_lent, near_lent)
    far_term = traded(mul_t(far_3, turned).astype(bf16), 3)
    last = turn(mixed, cosine_3, sine_3).astype(bf16)
    picked = jnp.stack([mul_t(select, last[:rows]), mul_t(select, last[rows:])])
    residual = picked - observed.astype(f32)
    adjoint = lax.optimization_barrier(mul_t(near_3, turned)) + far_term.astype(f32)
    turned = turn_back(adjoint, cosine_2, sine_2).astype(bf16)

    far_term = traded(mul_t(far_2, turned).astype(bf16), 2)
    adjoint = lax.optimization_barrier(mul_t(near_2, turned)) + far_term.astype(f32)
    turned = turn_back(adjoint, cosine_1, sine_1).astype(bf16)

    n_bfly, n_freq = lax.axis_size("bfly"), lax.axis_size("freq")
    inputs = (turned, near_1, far_1, near_0, far_0, waves_0, near_lent, far_lent, waves_lent)
    terms = pl.pallas_call(
        last_terms,
        out_shape=shape((4 * n_freq, 1, 2 * rows), f32),
        in_specs=[VMEM] * 13 + [SMEM],
        out_specs=VMEM,
        compiler_params=pltpu.CompilerParams(vmem_limit_bytes=16 << 20),
        name="last_terms",
    )(*map(in_vmem, (*inputs, sources, lent, across, across_lent)), (lax.axis_index("bfly") & 3)[None])
    groups = [
        [f * n_bfly + high + low for f in range(n_freq) for low in range(4)]
        for high in range(0, n_bfly, 4)
    ]
    terms = lax.all_to_all(terms, ("freq", "bfly"), 0, 0, axis_index_groups=groups)
    gradient = pl.pallas_call(
        last_ratio,
        out_shape=jax.ShapeDtypeStruct((1, rows), f32),
        in_specs=[VMEM],
        out_specs=VMEM,
        compiler_params=pltpu.CompilerParams(vmem_limit_bytes=16 << 20),
        name="last_ratio",
    )(in_vmem(terms))
    return (gradient[0], residual)


def solution(mesh):
    return jax.shard_map(
        local,
        mesh=mesh,
        in_specs=(
            P(None, "bfly", "freq"),
            P(None, "bfly", "freq"),
            P("bfly"),
            P("bfly"),
            P(None, "bfly", "freq"),
            P(None, None, "bfly", None),
            P(None, None, "bfly", None),
            P(None, None, "bfly", None),
        ),
        out_specs=(P("bfly"), P(None, "bfly", "freq")),
        check_vma=False,
    )
```

```python
import jax
import jax.numpy as jnp
from jax import lax
from jax.experimental import pallas as pl
from jax.experimental.pallas import tpu as pltpu
from jax.sharding import PartitionSpec as P

epsilon = 1e-05
bf16, f32 = jnp.bfloat16, jnp.float32
VMEM = pl.BlockSpec(memory_space=pltpu.VMEM)
SMEM = pl.BlockSpec(memory_space=pltpu.SMEM)


def swapped(block, stride):
    count = lax.axis_size("bfly")
    route = [(place, place ^ 1 << stride) for place in range(count)]
    return lax.ppermute(block, "bfly", route)


def traded(block, stride):
    count = lax.axis_size("bfly")
    pairs = [[low, low | 1 << stride] for low in range(count) if not low >> stride & 1]
    both = lax.all_gather(block, "bfly", axis_index_groups=pairs)
    return jnp.where((lax.axis_index("bfly") >> stride & 1) == 0, both[1], both[0])


def after(values, *done):
    return lax.optimization_barrier((values, *done))[0]


def stacked(block):
    real, imag = block[0], block[1]
    top = jnp.concatenate([real, -imag], axis=-1)
    bottom = jnp.concatenate([imag, real], axis=-1)
    return jnp.concatenate([top, bottom], axis=-2)


def mul(matrix, values):
    return jnp.dot(matrix, values, preferred_element_type=f32)


def mul_t(matrix, values):
    contract = (((0,), (0,)), ((), ()))
    return lax.dot_general(matrix, values, contract, preferred_element_type=f32)


def turn(values, cosine, sine):
    rows = values.shape[0] // 2
    real, imag = values[:rows], values[rows:]
    return jnp.concatenate([cosine * real - sine * imag, sine * real + cosine * imag])


def turn_back(values, cosine, sine):
    rows = values.shape[0] // 2
    real, imag = values[:rows], values[rows:]
    return jnp.concatenate([cosine * real + sine * imag, cosine * imag - sine * real])


def masked(blocks, pattern_ref, level, kind):
    rows = blocks.shape[-1]
    half = rows // 2

    def band(side):
        keep = [
            jnp.broadcast_to(pattern_ref[kind, side, part : part + 1, level : level + 1], (half, half))
            for part in range(2)
        ]
        return jnp.concatenate(keep, axis=1).astype(f32).astype(bf16)

    mask = jnp.concatenate([band(0), band(1)])
    return [blocks[part] * mask for part in range(2)]


def waves(angles, columns):
    count = angles.shape[0]
    both = jnp.concatenate([jnp.cos(angles), jnp.sin(angles)])
    place = lax.broadcasted_iota(jnp.int32, (2 * count, 2 * columns), 1) // (columns // count)
    pick = (place == lax.broadcasted_iota(jnp.int32, place.shape, 0)).astype(f32)
    contract = (((0,), (0,)), ((), ()))
    return lax.dot_general(
        both, pick, contract, precision=lax.Precision.HIGHEST, preferred_element_type=f32
    )


def first_field(sources_ref, model_ref, field_out):
    rows = model_ref.shape[-1]
    place = lax.broadcasted_iota(jnp.int32, (rows, rows), 0)
    diagonal = place == lax.broadcasted_iota(jnp.int32, (rows, rows), 1)
    factor = jnp.sum(jnp.where(diagonal, model_ref[...], 0.0), axis=1, keepdims=True)
    for part in range(2):
        field = factor * sources_ref[part].astype(f32)
        field_out[part * rows : (part + 1) * rows] = field.astype(bf16)


def first_maps(
    sources_ref, near_ref, far_ref, pattern_ref, phases_ref, near_out, far_out, waves_out, lend_out
):
    rows, columns = sources_ref.shape[1:]
    near = masked(near_ref[0], pattern_ref, 0, 0)
    far = masked(far_ref[0], pattern_ref, 0, 1)
    near_out[...] = stacked(near)
    far_out[...] = stacked(far)
    angles = phases_ref[0]
    waves_out[...] = waves(angles, columns)
    for part in range(2):
        lend_out[part * rows : (part + 1) * rows] = sources_ref[part]
        both = jnp.concatenate([near[part], far[part]], axis=1)
        lend_out[(2 + part) * rows : (3 + part) * rows] = both
    high = angles.astype(bf16).astype(f32)
    middle = (angles - high).astype(bf16).astype(f32)
    low = angles - high - middle
    low = jnp.concatenate([low, jnp.zeros_like(low)], axis=1)
    split = jnp.concatenate([jnp.concatenate([high, middle], axis=1), low])
    lend_out[4 * rows :] = jnp.concatenate([split, jnp.zeros_like(split)]).astype(bf16)


def lent_maps(lent_ref, near_out, far_out, waves_out):
    columns = lent_ref.shape[1]
    rows = near_out.shape[0] // 2
    split = lent_ref[4 * rows :].astype(f32)
    count = split.shape[0] // 4
    angles = split[:count, :rows] + split[:count, rows:] + split[count : 2 * count, :rows]
    waves_out[...] = waves(angles, columns)
    real, imag = lent_ref[2 * rows : 3 * rows], lent_ref[3 * rows : 4 * rows]
    near_out[...] = stacked([real[:, :rows], imag[:, :rows]])
    far_out[...] = stacked([real[:, rows:], imag[:, rows:]])


def middle_maps(near_ref, far_ref, pattern_ref, phases_ref, near_out, far_out, waves_out):
    near_out[...] = stacked(masked(near_ref[0], pattern_ref, 1, 0))
    far_out[...] = stacked(masked(far_ref[0], pattern_ref, 1, 1))
    waves_out[...] = waves(phases_ref[0], waves_out.shape[-1] // 2)


def later_maps(
    near_ref, far_ref, pattern_ref, phases_ref, observed_ref, receivers_ref,
    near_out, far_out, wide_out, waves_out, select_out, counts_out, data_out,
):
    rows, columns = observed_ref.shape[1:]
    for level in range(2, 4):
        near_out[level - 2] = stacked(masked(near_ref[level - 2], pattern_ref, level, 0))
        far_out[level - 2] = stacked(masked(far_ref[level - 2], pattern_ref, level, 1))
        wide_out[level - 2] = jnp.concatenate([far_out[level - 2], near_out[level - 2]], axis=1)
        waves_out[level - 2] = waves(phases_ref[level - 2], columns)
    select = receivers_ref[...] == lax.broadcasted_iota(jnp.int32, (rows, rows), 0)
    select = select.astype(f32)
    counts = jnp.broadcast_to(jnp.sum(select, axis=1, keepdims=True), (rows, columns))
    counts_out[...] = jnp.concatenate([counts, counts])
    select = select.astype(bf16)
    select_out[...] = select
    spread = jnp.concatenate([mul(select, observed_ref[0]), mul(select, observed_ref[1])])
    cosine, sine = waves_out[1, :, :columns], waves_out[1, :, columns:]
    data_out[...] = turn_back(spread, cosine, sine)


def last_terms(
    turned_ref, near_1_ref, far_1_ref, near_ref, far_ref, waves_ref, near_2_ref, far_2_ref,
    waves_2_ref, sources_ref, lent_ref, across_ref, across_lent_ref, place_ref, terms_out,
):
    rows = sources_ref.shape[0] // 2
    columns = sources_ref.shape[1]

    def row_sums(product):
        total = product[:rows] + product[rows:]
        total = total[:, : columns // 2] + total[:, columns // 2 :]
        return jnp.sum(total.T, axis=0, keepdims=True)

    def term(sources, maps_ref, turned):
        return row_sums(sources.astype(f32) * mul_t(maps_ref[...], turned))

    def turned_by(values, wave_ref):
        return turn_back(values, wave_ref[:, :columns], wave_ref[:, columns:]).astype(bf16)

    turned = turned_ref[...]
    own = turned_by(mul_t(near_1_ref[...], turned), waves_ref)
    other = turned_by(mul_t(far_1_ref[...], turned), waves_2_ref)
    terms = [
        term(sources_ref[...], near_ref, own),
        term(across_ref[...], far_ref, own),
        term(lent_ref[: 2 * rows], near_2_ref, other),
        term(across_lent_ref[...], far_2_ref, other),
    ]
    wide = sources_ref[...].astype(f32)
    light = row_sums(wide * wide)
    lights = [light] + [jnp.zeros_like(light)] * 3
    terms = [jnp.concatenate(pair, axis=1) for pair in zip(terms, lights)]
    for bit in (1, 2):
        swap = place_ref[0] & bit != 0
        terms = [jnp.where(swap, terms[n ^ bit], terms[n]) for n in range(4)]
    quad = jnp.concatenate(terms)
    n_freq = terms_out.shape[0] // 4
    terms_out[...] = jnp.concatenate([quad[None]] * n_freq).reshape(terms_out.shape)


def last_ratio(terms_ref, gradient_out):
    rows = gradient_out.shape[-1]
    total = jnp.sum(terms_ref[...], axis=0)
    gradient_out[...] = total[:, :rows] / jnp.sqrt(total[:, rows:] + epsilon)


def in_hbm(values):
    return pltpu.with_memory_space_constraint(values, pltpu.HBM)


def in_vmem(values):
    return pltpu.with_memory_space_constraint(values, pltpu.VMEM)


def local(sources, observed, receivers, model, phases, near_blocks, far_blocks, pattern):
    rows, columns = sources.shape[1:]
    shape = pltpu.VMEM
    phases = phases.transpose(0, 2, 1)
    pattern = pattern.transpose(1, 2, 3, 0)

    field = pl.pallas_call(
        first_field,
        out_shape=shape((2 * rows, columns), bf16),
        in_specs=[VMEM, VMEM],
        out_specs=VMEM,
        compiler_params=pltpu.CompilerParams(vmem_limit_bytes=16 << 20),
        name="first_field",
    )(in_hbm(sources), in_hbm(model[None]))
    partner = swapped(field, 0)
    blocks = pl.BlockSpec((1, 2, rows, rows), lambda step: (0, 0, 0, 0))
    angles = pl.BlockSpec((1, *phases.shape[1:]), lambda step: (0, 0, 0))
    near_0, far_0, waves_0, lend = pl.pallas_call(
        first_maps,
        out_shape=(
            shape((2 * rows, 2 * rows), bf16),
            shape((2 * rows, 2 * rows), bf16),
            shape((rows, 2 * columns), f32),
            shape((4 * rows + 16, columns), bf16),
        ),
        grid=(1,),
        in_specs=[VMEM, blocks, blocks, VMEM, angles],
        out_specs=(VMEM,) * 4,
        compiler_params=pltpu.CompilerParams(vmem_limit_bytes=16 << 20),
        name="first_maps",
    )(*map(in_hbm, (sources, near_blocks, far_blocks, pattern, phases)))
    cosine_0, sine_0 = waves_0[:, :columns], waves_0[:, columns:]
    mixed = mul(near_0, field) + mul(far_0, partner)
    field = turn(mixed, cosine_0, sine_0).astype(bf16)

    partner = swapped(field, 1)
    lent = swapped(after(lend, field), 1)
    blocks = pl.BlockSpec((1, 2, rows, rows), lambda step: (1, 0, 0, 0))
    angles = pl.BlockSpec((1, *phases.shape[1:]), lambda step: (1, 0, 0))
    near_1, far_1, waves_1 = pl.pallas_call(
        middle_maps,
        out_shape=(
            shape((2 * rows, 2 * rows), bf16),
            shape((2 * rows, 2 * rows), bf16),
            shape((rows, 2 * columns), f32),
        ),
        grid=(1,),
        in_specs=[blocks, blocks, VMEM, angles],
        out_specs=(VMEM,) * 3,
        compiler_params=pltpu.CompilerParams(vmem_limit_bytes=16 << 20),
        name="middle_maps",
    )(*map(in_hbm, (near_blocks, far_blocks)), after(pattern, field), in_hbm(phases))
    cosine_1, sine_1 = waves_1[:, :columns], waves_1[:, columns:]
    mixed = mul(near_1, field) + mul(far_1, partner)
    field = turn(mixed, cosine_1, sine_1).astype(bf16)

    partner = swapped(field, 2)
    blocks = pl.BlockSpec((2, 2, rows, rows), lambda step: (1, 0, 0, 0))
    angles = pl.BlockSpec((2, *phases.shape[1:]), lambda step: (1, 0, 0))
    near, far, wide, wave, select, counts, data = pl.pallas_call(
        later_maps,
        out_shape=(
            shape((2, 2 * rows, 2 * rows), bf16),
            shape((2, 2 * rows, 2 * rows), bf16),
            shape((2, 2 * rows, 4 * rows), bf16),
            shape((2, rows, 2 * columns), f32),
            shape((rows, rows), bf16),
            shape((2 * rows, columns), f32),
            shape((2 * rows, columns), f32),
        ),
        grid=(1,),
        in_specs=[blocks, blocks, VMEM, angles, VMEM, VMEM],
        out_specs=(VMEM,) * 7,
        compiler_params=pltpu.CompilerParams(vmem_limit_bytes=16 << 20),
        name="later_maps",
    )(
        *map(in_hbm, (near_blocks, far_blocks, pattern, phases, observed)),
        after(receivers, field)[None],
    )
    near_2, near_3 = near
    far_2, far_3 = far
    (cosine_2, sine_2), (cosine_3, sine_3) = (
        (each[:, :columns], each[:, columns:]) for each in wave
    )
    mixed = mul(near_2, field) + mul(far_2, partner)
    field = turn(mixed, cosine_2, sine_2).astype(bf16)

    partner = swapped(field, 3)
    sources = sources.reshape(2 * rows, columns)
    lent = after(lent, field)
    across, across_lent = swapped(after(sources, field), 0), swapped(lent[: 2 * rows], 0)
    near_lent, far_lent, waves_lent = pl.pallas_call(
        lent_maps,
        out_shape=(
            shape((2 * rows, 2 * rows), bf16),
            shape((2 * rows, 2 * rows), bf16),
            shape((rows, 2 * columns), f32),
        ),
        in_specs=[VMEM],
        out_specs=(VMEM,) * 3,
        compiler_params=pltpu.CompilerParams(vmem_limit_bytes=16 << 20),
        name="lent_maps",
    )(in_vmem(lent))
    mixed = mul(near_3, field) + mul(far_3, partner)
    turned = (counts * mixed - data).astype(bf16)

    turned = after(turned, across, across_lent, near_lent)
    both = lax.optimization_barrier(mul_t(wide[1], turned))
    far_term = traded(both[: 2 * rows].astype(bf16), 3)
    last = turn(mixed, cosine_3, sine_3).astype(bf16)
    picked = jnp.stack([mul_t(select, last[:rows]), mul_t(select, last[rows:])])
    residual = picked - observed.astype(f32)
    adjoint = both[2 * rows :] + far_term.astype(f32)
    turned = turn_back(adjoint, cosine_2, sine_2).astype(bf16)

    both = lax.optimization_barrier(mul_t(wide[0], turned))
    far_term = traded(both[: 2 * rows].astype(bf16), 2)
    adjoint = both[2 * rows :] + far_term.astype(f32)
    turned = turn_back(adjoint, cosine_1, sine_1).astype(bf16)

    n_bfly, n_freq = lax.axis_size("bfly"), lax.axis_size("freq")
    inputs = (turned, near_1, far_1, near_0, far_0, waves_0, near_lent, far_lent, waves_lent)
    terms = pl.pallas_call(
        last_terms,
        out_shape=shape((4 * n_freq, 1, 2 * rows), f32),
        in_specs=[VMEM] * 13 + [SMEM],
        out_specs=VMEM,
        compiler_params=pltpu.CompilerParams(vmem_limit_bytes=16 << 20),
        name="last_terms",
    )(*map(in_vmem, (*inputs, sources, lent, across, across_lent)), (lax.axis_index("bfly") & 3)[None])
    groups = [
        [f * n_bfly + high + low for f in range(n_freq) for low in range(4)]
        for high in range(0, n_bfly, 4)
    ]
    terms = lax.all_to_all(terms, ("freq", "bfly"), 0, 0, axis_index_groups=groups)
    gradient = pl.pallas_call(
        last_ratio,
        out_shape=jax.ShapeDtypeStruct((1, rows), f32),
        in_specs=[VMEM],
        out_specs=VMEM,
        compiler_params=pltpu.CompilerParams(vmem_limit_bytes=16 << 20),
        name="last_ratio",
    )(in_vmem(terms))
    return (gradient[0], residual)


def solution(mesh):
    return jax.shard_map(
        local,
        mesh=mesh,
        in_specs=(
            P(None, "bfly", "freq"),
            P(None, "bfly", "freq"),
            P("bfly"),
            P("bfly"),
            P(None, "bfly", "freq"),
            P(None, None, "bfly", None),
            P(None, None, "bfly", None),
            P(None, None, "bfly", None),
        ),
        out_specs=(P("bfly"), P(None, "bfly", "freq")),
        check_vma=False,
    )
```

```python
import jax
import jax.numpy as jnp
from jax import lax
from jax.experimental import pallas as pl
from jax.experimental.pallas import tpu as pltpu
from jax.sharding import PartitionSpec as P

epsilon = 1e-05
bf16, f32 = jnp.bfloat16, jnp.float32
VMEM = pl.BlockSpec(memory_space=pltpu.VMEM)
SMEM = pl.BlockSpec(memory_space=pltpu.SMEM)


def swapped(block, stride):
    count = lax.axis_size("bfly")
    route = [(place, place ^ 1 << stride) for place in range(count)]
    return lax.ppermute(block, "bfly", route)


def traded(block, stride):
    count = lax.axis_size("bfly")
    pairs = [[low, low | 1 << stride] for low in range(count) if not low >> stride & 1]
    both = lax.all_gather(block, "bfly", axis_index_groups=pairs)
    return jnp.where((lax.axis_index("bfly") >> stride & 1) == 0, both[1], both[0])


def after(values, *done):
    return lax.optimization_barrier((values, *done))[0]


def stacked(block):
    real, imag = block[0], block[1]
    top = jnp.concatenate([real, -imag], axis=-1)
    bottom = jnp.concatenate([imag, real], axis=-1)
    return jnp.concatenate([top, bottom], axis=-2)


def mul(matrix, values):
    return jnp.dot(matrix, values, preferred_element_type=f32)


def mul_t(matrix, values):
    contract = (((0,), (0,)), ((), ()))
    return lax.dot_general(matrix, values, contract, preferred_element_type=f32)


def turn(values, cosine, sine):
    rows = values.shape[0] // 2
    real, imag = values[:rows], values[rows:]
    return jnp.concatenate([cosine * real - sine * imag, sine * real + cosine * imag])


def turn_back(values, cosine, sine):
    rows = values.shape[0] // 2
    real, imag = values[:rows], values[rows:]
    return jnp.concatenate([cosine * real + sine * imag, cosine * imag - sine * real])


def masked(blocks, pattern_ref, level, kind):
    rows = blocks.shape[-1]
    half = rows // 2

    def band(side):
        keep = [
            jnp.broadcast_to(pattern_ref[kind, side, part : part + 1, level : level + 1], (half, half))
            for part in range(2)
        ]
        return jnp.concatenate(keep, axis=1).astype(f32).astype(bf16)

    mask = jnp.concatenate([band(0), band(1)])
    return [blocks[part] * mask for part in range(2)]


def waves(angles, columns):
    count = angles.shape[0]
    both = jnp.concatenate([jnp.cos(angles), jnp.sin(angles)])
    place = lax.broadcasted_iota(jnp.int32, (2 * count, 2 * columns), 1) // (columns // count)
    pick = (place == lax.broadcasted_iota(jnp.int32, place.shape, 0)).astype(f32)
    contract = (((0,), (0,)), ((), ()))
    return lax.dot_general(
        both, pick, contract, precision=lax.Precision.HIGHEST, preferred_element_type=f32
    )


def first_field(sources_ref, model_ref, field_out):
    rows = model_ref.shape[-1]
    place = lax.broadcasted_iota(jnp.int32, (rows, rows), 0)
    diagonal = place == lax.broadcasted_iota(jnp.int32, (rows, rows), 1)
    factor = jnp.sum(jnp.where(diagonal, model_ref[...], 0.0), axis=1, keepdims=True)
    for part in range(2):
        field = factor * sources_ref[part].astype(f32)
        field_out[part * rows : (part + 1) * rows] = field.astype(bf16)


def first_maps(
    sources_ref, near_ref, far_ref, pattern_ref, phases_ref, near_out, far_out, waves_out, lend_out
):
    rows, columns = sources_ref.shape[1:]
    near = masked(near_ref[0], pattern_ref, 0, 0)
    far = masked(far_ref[0], pattern_ref, 0, 1)
    near_out[...] = stacked(near)
    far_out[...] = stacked(far)
    angles = phases_ref[0]
    waves_out[...] = waves(angles, columns)
    for part in range(2):
        lend_out[part * rows : (part + 1) * rows] = sources_ref[part]
        both = jnp.concatenate([near[part], far[part]], axis=1)
        lend_out[(2 + part) * rows : (3 + part) * rows] = both
    high = angles.astype(bf16).astype(f32)
    middle = (angles - high).astype(bf16).astype(f32)
    low = angles - high - middle
    low = jnp.concatenate([low, jnp.zeros_like(low)], axis=1)
    split = jnp.concatenate([jnp.concatenate([high, middle], axis=1), low])
    lend_out[4 * rows :] = jnp.concatenate([split, jnp.zeros_like(split)]).astype(bf16)


def lent_maps(lent_ref, near_out, far_out, waves_out):
    columns = lent_ref.shape[1]
    rows = near_out.shape[0] // 2
    split = lent_ref[4 * rows :].astype(f32)
    count = split.shape[0] // 4
    angles = split[:count, :rows] + split[:count, rows:] + split[count : 2 * count, :rows]
    waves_out[...] = waves(angles, columns)
    real, imag = lent_ref[2 * rows : 3 * rows], lent_ref[3 * rows : 4 * rows]
    near_out[...] = stacked([real[:, :rows], imag[:, :rows]])
    far_out[...] = stacked([real[:, rows:], imag[:, rows:]])


def middle_maps(near_ref, far_ref, pattern_ref, phases_ref, near_out, far_out, waves_out):
    near_out[...] = stacked(masked(near_ref[0], pattern_ref, 1, 0))
    far_out[...] = stacked(masked(far_ref[0], pattern_ref, 1, 1))
    waves_out[...] = waves(phases_ref[0], waves_out.shape[-1] // 2)


def later_maps(
    near_ref, far_ref, pattern_ref, phases_ref, observed_ref, receivers_ref,
    near_out, far_out, waves_out, select_out, counts_out, data_out,
):
    rows, columns = observed_ref.shape[1:]
    for level in range(2, 4):
        near_out[level - 2] = stacked(masked(near_ref[level - 2], pattern_ref, level, 0))
        far_out[level - 2] = stacked(masked(far_ref[level - 2], pattern_ref, level, 1))
        waves_out[level - 2] = waves(phases_ref[level - 2], columns)
    select = receivers_ref[...] == lax.broadcasted_iota(jnp.int32, (rows, rows), 0)
    select = select.astype(f32)
    counts = jnp.broadcast_to(jnp.sum(select, axis=1, keepdims=True), (rows, columns))
    counts_out[...] = jnp.concatenate([counts, counts])
    select = select.astype(bf16)
    select_out[...] = select
    spread = jnp.concatenate([mul(select, observed_ref[0]), mul(select, observed_ref[1])])
    cosine, sine = waves_out[1, :, :columns], waves_out[1, :, columns:]
    data_out[...] = turn_back(spread, cosine, sine)


def last_terms(
    turned_ref, near_1_ref, far_1_ref, near_ref, far_ref, waves_ref, near_2_ref, far_2_ref,
    waves_2_ref, sources_ref, lent_ref, across_ref, across_lent_ref, place_ref, terms_out,
):
    rows = sources_ref.shape[0] // 2
    columns = sources_ref.shape[1]

    def row_sums(product):
        total = product[:rows] + product[rows:]
        total = total[:, : columns // 2] + total[:, columns // 2 :]
        return jnp.sum(total.T, axis=0, keepdims=True)

    def term(sources, maps_ref, turned):
        return row_sums(sources.astype(f32) * mul_t(maps_ref[...], turned))

    def turned_by(values, wave_ref):
        return turn_back(values, wave_ref[:, :columns], wave_ref[:, columns:]).astype(bf16)

    turned = turned_ref[...]
    own = turned_by(mul_t(near_1_ref[...], turned), waves_ref)
    other = turned_by(mul_t(far_1_ref[...], turned), waves_2_ref)
    terms = [
        term(sources_ref[...], near_ref, own),
        term(across_ref[...], far_ref, own),
        term(lent_ref[: 2 * rows], near_2_ref, other),
        term(across_lent_ref[...], far_2_ref, other),
    ]
    wide = sources_ref[...].astype(f32)
    light = row_sums(wide * wide)
    lights = [light] + [jnp.zeros_like(light)] * 3
    terms = [jnp.concatenate(pair, axis=1) for pair in zip(terms, lights)]
    for bit in (1, 2):
        swap = place_ref[0] & bit != 0
        terms = [jnp.where(swap, terms[n ^ bit], terms[n]) for n in range(4)]
    quad = jnp.concatenate(terms)
    n_freq = terms_out.shape[0] // 4
    terms_out[...] = jnp.concatenate([quad[None]] * n_freq).reshape(terms_out.shape)


def last_ratio(terms_ref, gradient_out):
    rows = gradient_out.shape[-1]
    total = jnp.sum(terms_ref[...], axis=0)
    gradient_out[...] = total[:, :rows] / jnp.sqrt(total[:, rows:] + epsilon)


def in_hbm(values):
    return pltpu.with_memory_space_constraint(values, pltpu.HBM)


def in_vmem(values):
    return pltpu.with_memory_space_constraint(values, pltpu.VMEM)


def local(sources, observed, receivers, model, phases, near_blocks, far_blocks, pattern):
    rows, columns = sources.shape[1:]
    shape = pltpu.VMEM
    phases = phases.transpose(0, 2, 1)
    pattern = pattern.transpose(1, 2, 3, 0)

    field = pl.pallas_call(
        first_field,
        out_shape=shape((2 * rows, columns), bf16),
        in_specs=[VMEM, VMEM],
        out_specs=VMEM,
        compiler_params=pltpu.CompilerParams(vmem_limit_bytes=16 << 20),
        name="first_field",
    )(in_hbm(sources), in_hbm(model[None]))
    partner = swapped(field, 0)
    blocks = pl.BlockSpec((1, 2, rows, rows), lambda step: (0, 0, 0, 0))
    angles = pl.BlockSpec((1, *phases.shape[1:]), lambda step: (0, 0, 0))
    near_0, far_0, waves_0, lend = pl.pallas_call(
        first_maps,
        out_shape=(
            shape((2 * rows, 2 * rows), bf16),
            shape((2 * rows, 2 * rows), bf16),
            shape((rows, 2 * columns), f32),
            shape((4 * rows + 16, columns), bf16),
        ),
        grid=(1,),
        in_specs=[VMEM, blocks, blocks, VMEM, angles],
        out_specs=(VMEM,) * 4,
        compiler_params=pltpu.CompilerParams(vmem_limit_bytes=16 << 20),
        name="first_maps",
    )(*map(in_hbm, (sources, near_blocks, far_blocks, pattern, phases)))
    cosine_0, sine_0 = waves_0[:, :columns], waves_0[:, columns:]
    mixed = mul(near_0, field) + mul(far_0, partner)
    field = turn(mixed, cosine_0, sine_0).astype(bf16)

    partner = swapped(field, 1)
    lent = swapped(after(lend, field), 1)
    blocks = pl.BlockSpec((1, 2, rows, rows), lambda step: (1, 0, 0, 0))
    angles = pl.BlockSpec((1, *phases.shape[1:]), lambda step: (1, 0, 0))
    near_1, far_1, waves_1 = pl.pallas_call(
        middle_maps,
        out_shape=(
            shape((2 * rows, 2 * rows), bf16),
            shape((2 * rows, 2 * rows), bf16),
            shape((rows, 2 * columns), f32),
        ),
        grid=(1,),
        in_specs=[blocks, blocks, VMEM, angles],
        out_specs=(VMEM,) * 3,
        compiler_params=pltpu.CompilerParams(vmem_limit_bytes=16 << 20),
        name="middle_maps",
    )(*map(in_hbm, (near_blocks, far_blocks)), after(pattern, field), in_hbm(phases))
    cosine_1, sine_1 = waves_1[:, :columns], waves_1[:, columns:]
    mixed = mul(near_1, field) + mul(far_1, partner)
    field = turn(mixed, cosine_1, sine_1).astype(bf16)

    partner = swapped(field, 2)
    blocks = pl.BlockSpec((2, 2, rows, rows), lambda step: (1, 0, 0, 0))
    angles = pl.BlockSpec((2, *phases.shape[1:]), lambda step: (1, 0, 0))
    near, far, wave, select, counts, data = pl.pallas_call(
        later_maps,
        out_shape=(
            shape((2, 2 * rows, 2 * rows), bf16),
            shape((2, 2 * rows, 2 * rows), bf16),
            shape((2, rows, 2 * columns), f32),
            shape((rows, rows), bf16),
            shape((2 * rows, columns), f32),
            shape((2 * rows, columns), f32),
        ),
        grid=(1,),
        in_specs=[blocks, blocks, VMEM, angles, VMEM, VMEM],
        out_specs=(VMEM,) * 6,
        compiler_params=pltpu.CompilerParams(vmem_limit_bytes=16 << 20),
        name="later_maps",
    )(
        *map(in_hbm, (near_blocks, far_blocks, pattern, phases, observed)),
        after(receivers, field)[None],
    )
    near_2, near_3 = near
    far_2, far_3 = far
    (cosine_2, sine_2), (cosine_3, sine_3) = (
        (each[:, :columns], each[:, columns:]) for each in wave
    )
    mixed = mul(near_2, field) + mul(far_2, partner)
    field = turn(mixed, cosine_2, sine_2).astype(bf16)

    partner = swapped(field, 3)
    sources = sources.reshape(2 * rows, columns)
    lent = after(lent, field)
    across, across_lent = swapped(after(sources, field), 0), swapped(lent[: 2 * rows], 0)
    near_lent, far_lent, waves_lent = pl.pallas_call(
        lent_maps,
        out_shape=(
            shape((2 * rows, 2 * rows), bf16),
            shape((2 * rows, 2 * rows), bf16),
            shape((rows, 2 * columns), f32),
        ),
        in_specs=[VMEM],
        out_specs=(VMEM,) * 3,
        compiler_params=pltpu.CompilerParams(vmem_limit_bytes=16 << 20),
        name="lent_maps",
    )(in_vmem(lent))
    mixed = mul(near_3, field) + mul(far_3, partner)
    turned = (counts * mixed - data).astype(bf16)

    turned = after(turned, across, across_lent, near_lent)
    far_term = traded(mul_t(far_3, turned).astype(bf16), 3)
    last = turn(mixed, cosine_3, sine_3).astype(bf16)
    picked = jnp.stack([mul_t(select, last[:rows]), mul_t(select, last[rows:])])
    residual = picked - observed.astype(f32)
    adjoint = lax.optimization_barrier(mul_t(near_3, turned)) + far_term.astype(f32)
    turned = turn_back(adjoint, cosine_2, sine_2).astype(bf16)

    far_term = swapped(mul_t(far_2, turned).astype(bf16), 2)
    adjoint = lax.optimization_barrier(mul_t(near_2, turned)) + far_term.astype(f32)
    turned = turn_back(adjoint, cosine_1, sine_1).astype(bf16)

    n_bfly, n_freq = lax.axis_size("bfly"), lax.axis_size("freq")
    inputs = (turned, near_1, far_1, near_0, far_0, waves_0, near_lent, far_lent, waves_lent)
    terms = pl.pallas_call(
        last_terms,
        out_shape=shape((4 * n_freq, 1, 2 * rows), f32),
        in_specs=[VMEM] * 13 + [SMEM],
        out_specs=VMEM,
        compiler_params=pltpu.CompilerParams(vmem_limit_bytes=16 << 20),
        name="last_terms",
    )(*map(in_vmem, (*inputs, sources, lent, across, across_lent)), (lax.axis_index("bfly") & 3)[None])
    groups = [
        [f * n_bfly + high + low for f in range(n_freq) for low in range(4)]
        for high in range(0, n_bfly, 4)
    ]
    terms = lax.all_to_all(terms, ("freq", "bfly"), 0, 0, axis_index_groups=groups)
    gradient = pl.pallas_call(
        last_ratio,
        out_shape=jax.ShapeDtypeStruct((1, rows), f32),
        in_specs=[VMEM],
        out_specs=VMEM,
        compiler_params=pltpu.CompilerParams(vmem_limit_bytes=16 << 20),
        name="last_ratio",
    )(in_vmem(terms))
    return (gradient[0], residual)


def solution(mesh):
    return jax.shard_map(
        local,
        mesh=mesh,
        in_specs=(
            P(None, "bfly", "freq"),
            P(None, "bfly", "freq"),
            P("bfly"),
            P("bfly"),
            P(None, "bfly", "freq"),
            P(None, None, "bfly", None),
            P(None, None, "bfly", None),
            P(None, None, "bfly", None),
        ),
        out_specs=(P("bfly"), P(None, "bfly", "freq")),
        check_vma=False,
    )
```

```python
import jax
import jax.numpy as jnp
from jax import lax
from jax.experimental import pallas as pl
from jax.experimental.pallas import tpu as pltpu
from jax.sharding import PartitionSpec as P

epsilon = 1e-05
bf16, f32 = jnp.bfloat16, jnp.float32
VMEM = pl.BlockSpec(memory_space=pltpu.VMEM)
SMEM = pl.BlockSpec(memory_space=pltpu.SMEM)


def swapped(block, stride):
    count = lax.axis_size("bfly")
    route = [(place, place ^ 1 << stride) for place in range(count)]
    return lax.ppermute(block, "bfly", route)


def traded(block, stride):
    count = lax.axis_size("bfly")
    pairs = [[low, low | 1 << stride] for low in range(count) if not low >> stride & 1]
    both = lax.all_gather(block, "bfly", axis_index_groups=pairs)
    return jnp.where((lax.axis_index("bfly") >> stride & 1) == 0, both[1], both[0])


def after(values, *done):
    return lax.optimization_barrier((values, *done))[0]


def stacked(block):
    real, imag = block[0], block[1]
    top = jnp.concatenate([real, -imag], axis=-1)
    bottom = jnp.concatenate([imag, real], axis=-1)
    return jnp.concatenate([top, bottom], axis=-2)


def mul(matrix, values):
    return jnp.dot(matrix, values, preferred_element_type=f32)


def mul_t(matrix, values):
    contract = (((0,), (0,)), ((), ()))
    return lax.dot_general(matrix, values, contract, preferred_element_type=f32)


def turn(values, cosine, sine):
    rows = values.shape[0] // 2
    real, imag = values[:rows], values[rows:]
    return jnp.concatenate([cosine * real - sine * imag, sine * real + cosine * imag])


def turn_back(values, cosine, sine):
    rows = values.shape[0] // 2
    real, imag = values[:rows], values[rows:]
    return jnp.concatenate([cosine * real + sine * imag, cosine * imag - sine * real])


def masked(blocks, pattern_ref, level, kind):
    rows = blocks.shape[-1]
    half = rows // 2

    def band(side):
        keep = [
            jnp.broadcast_to(pattern_ref[kind, side, part : part + 1, level : level + 1], (half, half))
            for part in range(2)
        ]
        return jnp.concatenate(keep, axis=1).astype(f32).astype(bf16)

    mask = jnp.concatenate([band(0), band(1)])
    return [blocks[part] * mask for part in range(2)]


def waves(angles, columns):
    count = angles.shape[0]
    both = jnp.concatenate([jnp.cos(angles), jnp.sin(angles)])
    place = lax.broadcasted_iota(jnp.int32, (2 * count, 2 * columns), 1) // (columns // count)
    pick = (place == lax.broadcasted_iota(jnp.int32, place.shape, 0)).astype(f32)
    contract = (((0,), (0,)), ((), ()))
    return lax.dot_general(
        both, pick, contract, precision=lax.Precision.HIGHEST, preferred_element_type=f32
    )


def first_field(sources_ref, model_ref, field_out):
    rows = model_ref.shape[-1]
    place = lax.broadcasted_iota(jnp.int32, (rows, rows), 0)
    diagonal = place == lax.broadcasted_iota(jnp.int32, (rows, rows), 1)
    factor = jnp.sum(jnp.where(diagonal, model_ref[...], 0.0), axis=1, keepdims=True)
    for part in range(2):
        field = factor * sources_ref[part].astype(f32)
        field_out[part * rows : (part + 1) * rows] = field.astype(bf16)


def first_maps(
    sources_ref, near_ref, far_ref, pattern_ref, phases_ref, near_out, far_out, waves_out, lend_out
):
    rows, columns = sources_ref.shape[1:]
    near = masked(near_ref[0], pattern_ref, 0, 0)
    far = masked(far_ref[0], pattern_ref, 0, 1)
    near_out[...] = stacked(near)
    far_out[...] = stacked(far)
    angles = phases_ref[0]
    waves_out[...] = waves(angles, columns)
    for part in range(2):
        lend_out[part * rows : (part + 1) * rows] = sources_ref[part]
        both = jnp.concatenate([near[part], far[part]], axis=1)
        lend_out[(2 + part) * rows : (3 + part) * rows] = both
    high = angles.astype(bf16).astype(f32)
    middle = (angles - high).astype(bf16).astype(f32)
    low = angles - high - middle
    low = jnp.concatenate([low, jnp.zeros_like(low)], axis=1)
    split = jnp.concatenate([jnp.concatenate([high, middle], axis=1), low])
    lend_out[4 * rows :] = jnp.concatenate([split, jnp.zeros_like(split)]).astype(bf16)


def lent_maps(lent_ref, near_out, far_out, waves_out):
    columns = lent_ref.shape[1]
    rows = near_out.shape[0] // 2
    split = lent_ref[4 * rows :].astype(f32)
    count = split.shape[0] // 4
    angles = split[:count, :rows] + split[:count, rows:] + split[count : 2 * count, :rows]
    waves_out[...] = waves(angles, columns)
    real, imag = lent_ref[2 * rows : 3 * rows], lent_ref[3 * rows : 4 * rows]
    near_out[...] = stacked([real[:, :rows], imag[:, :rows]])
    far_out[...] = stacked([real[:, rows:], imag[:, rows:]])


def middle_maps(near_ref, far_ref, pattern_ref, phases_ref, near_out, far_out, waves_out):
    near_out[...] = stacked(masked(near_ref[0], pattern_ref, 1, 0))
    far_out[...] = stacked(masked(far_ref[0], pattern_ref, 1, 1))
    waves_out[...] = waves(phases_ref[0], waves_out.shape[-1] // 2)


def later_maps(
    near_ref, far_ref, pattern_ref, phases_ref, observed_ref, receivers_ref,
    near_out, far_out, waves_out, select_out, counts_out, data_out,
):
    rows, columns = observed_ref.shape[1:]
    for level in range(2, 4):
        near_out[level - 2] = stacked(masked(near_ref[level - 2], pattern_ref, level, 0))
        far_out[level - 2] = stacked(masked(far_ref[level - 2], pattern_ref, level, 1))
        waves_out[level - 2] = waves(phases_ref[level - 2], columns)
    select = receivers_ref[...] == lax.broadcasted_iota(jnp.int32, (rows, rows), 0)
    select = select.astype(f32)
    counts = jnp.broadcast_to(jnp.sum(select, axis=1, keepdims=True), (rows, columns))
    counts_out[...] = jnp.concatenate([counts, counts])
    select = select.astype(bf16)
    select_out[...] = select
    spread = jnp.concatenate([mul(select, observed_ref[0]), mul(select, observed_ref[1])])
    cosine, sine = waves_out[1, :, :columns], waves_out[1, :, columns:]
    data_out[...] = turn_back(spread, cosine, sine)


def last_terms(
    turned_ref, near_1_ref, far_1_ref, near_ref, far_ref, waves_ref, near_2_ref, far_2_ref,
    waves_2_ref, sources_ref, lent_ref, across_ref, across_lent_ref, place_ref, terms_out,
):
    rows = sources_ref.shape[0] // 2
    columns = sources_ref.shape[1]

    def row_sums(product):
        total = product[:rows] + product[rows:]
        total = total[:, : columns // 2] + total[:, columns // 2 :]
        return jnp.sum(total.T, axis=0, keepdims=True)

    def term(sources, maps_ref, turned):
        return row_sums(sources.astype(f32) * mul_t(maps_ref[...], turned))

    def turned_by(values, wave_ref):
        return turn_back(values, wave_ref[:, :columns], wave_ref[:, columns:]).astype(bf16)

    turned = turned_ref[...]
    own = turned_by(mul_t(near_1_ref[...], turned), waves_ref)
    other = turned_by(mul_t(far_1_ref[...], turned), waves_2_ref)
    terms = [
        term(sources_ref[...], near_ref, own),
        term(across_ref[...], far_ref, own),
        term(lent_ref[: 2 * rows], near_2_ref, other),
        term(across_lent_ref[...], far_2_ref, other),
    ]
    wide = sources_ref[...].astype(f32)
    light = row_sums(wide * wide)
    lights = [light] + [jnp.zeros_like(light)] * 3
    terms = [jnp.concatenate(pair, axis=1) for pair in zip(terms, lights)]
    for bit in (1, 2):
        swap = place_ref[0] & bit != 0
        terms = [jnp.where(swap, terms[n ^ bit], terms[n]) for n in range(4)]
    quad = jnp.concatenate(terms)
    n_freq = terms_out.shape[0] // 4
    terms_out[...] = jnp.concatenate([quad[None]] * n_freq).reshape(terms_out.shape)


def last_ratio(terms_ref, gradient_out):
    rows = gradient_out.shape[-1]
    total = jnp.sum(terms_ref[...], axis=0)
    gradient_out[...] = total[:, :rows] / jnp.sqrt(total[:, rows:] + epsilon)


def in_hbm(values):
    return pltpu.with_memory_space_constraint(values, pltpu.HBM)


def in_vmem(values):
    return pltpu.with_memory_space_constraint(values, pltpu.VMEM)


def local(sources, observed, receivers, model, phases, near_blocks, far_blocks, pattern):
    rows, columns = sources.shape[1:]
    shape = pltpu.VMEM
    phases = phases.transpose(0, 2, 1)
    pattern = pattern.transpose(1, 2, 3, 0)

    field = pl.pallas_call(
        first_field,
        out_shape=shape((2 * rows, columns), bf16),
        in_specs=[VMEM, VMEM],
        out_specs=VMEM,
        compiler_params=pltpu.CompilerParams(vmem_limit_bytes=16 << 20),
        name="first_field",
    )(in_hbm(sources), in_hbm(model[None]))
    partner = swapped(field, 0)
    blocks = pl.BlockSpec((1, 2, rows, rows), lambda step: (0, 0, 0, 0))
    angles = pl.BlockSpec((1, *phases.shape[1:]), lambda step: (0, 0, 0))
    near_0, far_0, waves_0, lend = pl.pallas_call(
        first_maps,
        out_shape=(
            shape((2 * rows, 2 * rows), bf16),
            shape((2 * rows, 2 * rows), bf16),
            shape((rows, 2 * columns), f32),
            shape((4 * rows + 16, columns), bf16),
        ),
        grid=(1,),
        in_specs=[VMEM, blocks, blocks, VMEM, angles],
        out_specs=(VMEM,) * 4,
        compiler_params=pltpu.CompilerParams(vmem_limit_bytes=16 << 20),
        name="first_maps",
    )(*map(in_hbm, (sources, near_blocks, far_blocks, pattern, phases)))
    cosine_0, sine_0 = waves_0[:, :columns], waves_0[:, columns:]
    mixed = mul(near_0, field) + mul(far_0, partner)
    field = turn(mixed, cosine_0, sine_0).astype(bf16)

    partner = swapped(field, 1)
    lent = swapped(after(lend, field), 1)
    blocks = pl.BlockSpec((1, 2, rows, rows), lambda step: (1, 0, 0, 0))
    angles = pl.BlockSpec((1, *phases.shape[1:]), lambda step: (1, 0, 0))
    near_1, far_1, waves_1 = pl.pallas_call(
        middle_maps,
        out_shape=(
            shape((2 * rows, 2 * rows), bf16),
            shape((2 * rows, 2 * rows), bf16),
            shape((rows, 2 * columns), f32),
        ),
        grid=(1,),
        in_specs=[blocks, blocks, VMEM, angles],
        out_specs=(VMEM,) * 3,
        compiler_params=pltpu.CompilerParams(vmem_limit_bytes=16 << 20),
        name="middle_maps",
    )(*map(in_hbm, (near_blocks, far_blocks)), after(pattern, field), in_hbm(phases))
    cosine_1, sine_1 = waves_1[:, :columns], waves_1[:, columns:]
    mixed = mul(near_1, field) + mul(far_1, partner)
    field = turn(mixed, cosine_1, sine_1).astype(bf16)

    partner = traded(field, 2)
    blocks = pl.BlockSpec((2, 2, rows, rows), lambda step: (1, 0, 0, 0))
    angles = pl.BlockSpec((2, *phases.shape[1:]), lambda step: (1, 0, 0))
    near, far, wave, select, counts, data = pl.pallas_call(
        later_maps,
        out_shape=(
            shape((2, 2 * rows, 2 * rows), bf16),
            shape((2, 2 * rows, 2 * rows), bf16),
            shape((2, rows, 2 * columns), f32),
            shape((rows, rows), bf16),
            shape((2 * rows, columns), f32),
            shape((2 * rows, columns), f32),
        ),
        grid=(1,),
        in_specs=[blocks, blocks, VMEM, angles, VMEM, VMEM],
        out_specs=(VMEM,) * 6,
        compiler_params=pltpu.CompilerParams(vmem_limit_bytes=16 << 20),
        name="later_maps",
    )(
        *map(in_hbm, (near_blocks, far_blocks, pattern, phases, observed)),
        after(receivers, field)[None],
    )
    near_2, near_3 = near
    far_2, far_3 = far
    (cosine_2, sine_2), (cosine_3, sine_3) = (
        (each[:, :columns], each[:, columns:]) for each in wave
    )
    mixed = mul(near_2, field) + mul(far_2, partner)
    field = turn(mixed, cosine_2, sine_2).astype(bf16)

    partner = swapped(field, 3)
    sources = sources.reshape(2 * rows, columns)
    lent = after(lent, field)
    across, across_lent = swapped(after(sources, field), 0), swapped(lent[: 2 * rows], 0)
    near_lent, far_lent, waves_lent = pl.pallas_call(
        lent_maps,
        out_shape=(
            shape((2 * rows, 2 * rows), bf16),
            shape((2 * rows, 2 * rows), bf16),
            shape((rows, 2 * columns), f32),
        ),
        in_specs=[VMEM],
        out_specs=(VMEM,) * 3,
        compiler_params=pltpu.CompilerParams(vmem_limit_bytes=16 << 20),
        name="lent_maps",
    )(in_vmem(lent))
    mixed = mul(near_3, field) + mul(far_3, partner)
    turned = (counts * mixed - data).astype(bf16)

    turned = after(turned, across, across_lent, near_lent)
    far_term = traded(mul_t(far_3, turned).astype(bf16), 3)
    last = turn(mixed, cosine_3, sine_3).astype(bf16)
    picked = jnp.stack([mul_t(select, last[:rows]), mul_t(select, last[rows:])])
    residual = picked - observed.astype(f32)
    adjoint = lax.optimization_barrier(mul_t(near_3, turned)) + far_term.astype(f32)
    turned = turn_back(adjoint, cosine_2, sine_2).astype(bf16)

    far_term = traded(mul_t(far_2, turned).astype(bf16), 2)
    adjoint = lax.optimization_barrier(mul_t(near_2, turned)) + far_term.astype(f32)
    turned = turn_back(adjoint, cosine_1, sine_1).astype(bf16)

    n_bfly, n_freq = lax.axis_size("bfly"), lax.axis_size("freq")
    inputs = (turned, near_1, far_1, near_0, far_0, waves_0, near_lent, far_lent, waves_lent)
    terms = pl.pallas_call(
        last_terms,
        out_shape=shape((4 * n_freq, 1, 2 * rows), f32),
        in_specs=[VMEM] * 13 + [SMEM],
        out_specs=VMEM,
        compiler_params=pltpu.CompilerParams(vmem_limit_bytes=16 << 20),
        name="last_terms",
    )(*map(in_vmem, (*inputs, sources, lent, across, across_lent)), (lax.axis_index("bfly") & 3)[None])
    groups = [
        [f * n_bfly + high + low for f in range(n_freq) for low in range(4)]
        for high in range(0, n_bfly, 4)
    ]
    terms = lax.all_to_all(terms, ("freq", "bfly"), 0, 0, axis_index_groups=groups)
    gradient = pl.pallas_call(
        last_ratio,
        out_shape=jax.ShapeDtypeStruct((1, rows), f32),
        in_specs=[VMEM],
        out_specs=VMEM,
        compiler_params=pltpu.CompilerParams(vmem_limit_bytes=16 << 20),
        name="last_ratio",
    )(in_vmem(terms))
    return (gradient[0], residual)


def solution(mesh):
    return jax.shard_map(
        local,
        mesh=mesh,
        in_specs=(
            P(None, "bfly", "freq"),
            P(None, "bfly", "freq"),
            P("bfly"),
            P("bfly"),
            P(None, "bfly", "freq"),
            P(None, None, "bfly", None),
            P(None, None, "bfly", None),
            P(None, None, "bfly", None),
        ),
        out_specs=(P("bfly"), P(None, "bfly", "freq")),
        check_vma=False,
    )
```
